32 devices in a mesh: group: 4 (over y, core), dev: 8 (over z, x).
Axes of the slice: x: 2, y: 2, z: 4, core: 2. Of those that a mesh axis runs over, the one named last changes fastest.
Arguments:
- schur: float32 [32, 1024, 1024], P(('group', 'dev'))
- coarse_modes: float32 [32, 6, 512], P(('group', 'dev')), may hold values from -4 to 4
- load: float32 [32, 64, 512], P(('group', 'dev')), may hold values from -6 to 6
- warm_start: float32 [32, 64, 512], P(('group', 'dev')), may hold values from -0.6 to 0.6
- active_blocks: int32 [32], P(('group', 'dev')), may hold values from 1 to 4, as said below
- contact_from: int32 [32], P(('group', 'dev')), may hold values from 0 to 127
Outputs:
- multipliers: float32 [32, 64, 512], P(('group', 'dev'))
- residual: float32 [32, 64, 512], P(('group', 'dev'))
- amplitudes: float32 [64, 6], replicated
The draws below stay inside these ranges and needn't reach their ends.
Inputs may be any that keep to these rules, and one draw needn't show every extreme that they name: Interface s carries multipliers on its first active_blocks[s] * 128 dofs only; some interface has 1 block and some has all.
All inputs are finite; a program needn't handle non-finite values.
Results may differ from the reference program's by a relative error of at most 0.00023.
Values sent between devices are 32-bit elements; how exact they have to be, the bound alone decides.
No kernel may reach another device: no remote copies, remote signals or barrier semaphores. Data moves between devices by JAX's collectives and lax.ppermute only.
A program may use at most 64 MiB of HBM per device.

```python
import math
import jax
import jax.numpy as jnp
from jax import lax

H = 512
M = 1024
BLK = 128
K = 64
NC = 6
ITERS = 3
SUBS = 32


def draw_schur(key, part):
    off_key, diag_key = jax.random.split(jax.random.fold_in(key, 11))
    spread = jax.random.normal(off_key, (SUBS, M, M), jnp.float32)
    diagonal = jax.random.uniform(diag_key, (SUBS, M), jnp.float32, 1.5, 2.5)
    spread = spread * (0.45 / math.sqrt(M))
    symmetric = (spread + jnp.swapaxes(spread, 1, 2)) / math.sqrt(2.0)
    identity = jnp.eye(M, dtype=jnp.float32)
    return symmetric * (1.0 - identity) + diagonal[:, :, None] * identity


def draw_active_blocks(key, part):
    first_key, second_key = jax.random.split(jax.random.fold_in(key, 23))
    levels = jax.random.randint(first_key, (SUBS,), 0, 4)
    blocks = jnp.where(levels == 3, H // BLK, jnp.where(levels == 2, 2, 1))
    order = jax.random.permutation(second_key, SUBS)
    blocks = blocks.at[order[0]].set(H // BLK)
    blocks = blocks.at[order[1]].set(1)
    return blocks.astype(jnp.int32)


def coarse_traces(key):
    rough_key = jax.random.fold_in(key, 31)
    across = ((jnp.arange(SUBS, dtype=jnp.float32) + 0.5) / SUBS * 2.0 - 1.0)[:, None]
    along_dof = ((jnp.arange(H, dtype=jnp.float32) + 0.5) / H * 2.0 - 1.0)[None, :]
    plane = jnp.zeros((SUBS, H), jnp.float32)
    smooth = jnp.stack([plane + 1.0, plane + across, plane + along_dof, across * along_dof, plane + jnp.cos(math.pi * across), plane + jnp.sin(math.pi * along_dof)], axis=1)
    rough_part = jnp.clip(0.7 * jax.random.normal(rough_key, (SUBS, NC, H), jnp.float32), -2.5, 2.5)
    return jnp.clip(smooth + rough_part, -4.0, 4.0)


def draw_coarse_modes(key, part):
    return coarse_traces(key)


def draw_load(key, part):
    traces = coarse_traces(key)
    jitter_key = jax.random.fold_in(key, 41)
    weight_key = jax.random.fold_in(key, 43)
    jitter = 0.8 * jax.random.normal(jitter_key, (SUBS, K, H), jnp.float32)
    weights = jax.random.uniform(weight_key, (K, NC), jnp.float32, -0.6, 0.6)
    summed = jitter
    for mode_index in range(NC):
        summed = summed + weights[None, :, mode_index, None] * traces[:, mode_index, None, :]
    return jnp.clip(summed, -6.0, 6.0)


def set_ends(array, rng, least, high):
    longest = array.shape.index(max(array.shape))
    spots = []
    for shift in (0, 1):
        where = [jax.random.randint(jax.random.fold_in(rng, axis), (), 0, length) for axis, length in enumerate(array.shape)]
        where[longest] = (where[longest] + shift) % array.shape[longest]
        spots.append(tuple(where))
    return array.at[spots[0]].set(least).at[spots[1]].set(high)


def shard_levels(key, shape, cuts, low, top_value):
    def one(axis_at, parts):
        draws = jax.random.uniform(jax.random.fold_in(jax.random.fold_in(key, 6), axis_at), (parts,), jnp.float32, low / len(cuts), top_value / len(cuts))
        return jnp.repeat(jnp.exp(draws), shape[axis_at] // parts).reshape((-1,) + (1,) * (len(shape) - axis_at - 1))

    factor_of = one(*cuts[0])
    for cut in cuts[1:]:
        factor_of = factor_of * one(*cut)
    return factor_of


def normal_values(key, extent, scale, limit, shards=(), held_as=jnp.bfloat16):
    array = scale * jax.random.normal(key, extent, jnp.float32)
    if shards:
        array = array * shard_levels(key, extent, shards, -0.22, 0.18)
    return jnp.clip(array, -limit, limit).astype(held_as)


def setup_inputs(seed: int = 0) -> dict:
    splits = jax.random.split(jax.random.key(seed), 7)
    schur = draw_schur(jax.random.fold_in(splits[6], 71), 0)
    coarse_modes = draw_coarse_modes(jax.random.fold_in(splits[6], 71), 0)
    load = draw_load(jax.random.fold_in(splits[6], 71), 0)
    warm_start = normal_values(splits[3], (SUBS, K, H), 0.1, 0.6, ((0, 32),), jnp.float32)
    active_blocks = draw_active_blocks(jax.random.fold_in(splits[6], 71), 0)
    contact_from = set_ends(jax.random.randint(splits[5], (SUBS,), 0, BLK), jax.random.fold_in(splits[5], 1), 0, BLK - 1).astype(jnp.int32)
    return dict(schur=schur, coarse_modes=coarse_modes, load=load, warm_start=warm_start, active_blocks=active_blocks, contact_from=contact_from)


LOWER = 0.1
UPPER = 8.0

def apply_dual(multipliers, schur):
    width = multipliers.shape[2]
    zeros = jnp.zeros((1,) + multipliers.shape[1:], jnp.float32)
    before = jnp.concatenate([zeros, multipliers[:-1]], axis=0)
    operand = jnp.concatenate([-before, multipliers], axis=2)
    product = jnp.einsum('skm,smn->skn', operand, schur, precision=lax.Precision.HIGHEST)
    after = jnp.concatenate([product[1:, :, :width], zeros], axis=0)
    return product[:, :, width:] - after

def coarse_solve(factor, coefficients):
    inner = lax.linalg.triangular_solve(factor, coefficients.T, left_side=True, lower=True)
    outer = lax.linalg.triangular_solve(factor, inner, left_side=True, lower=True, transpose_a=True)
    return outer.T

def reference(schur, coarse_modes, load, warm_start, active_blocks, contact_from):
    width = load.shape[2]
    dofs = lax.broadcasted_iota(jnp.int32, (load.shape[0], width), 1)
    alive = dofs < (active_blocks * BLK)[:, None]
    live = alive.astype(jnp.float32)
    contact = (alive & (dofs >= contact_from[:, None]))[:, None, :]
    modes = coarse_modes * live[:, None, :]
    gram = jnp.einsum('sch,seh->ce', modes, modes, precision=lax.Precision.HIGHEST)
    factor = jnp.linalg.cholesky(gram)
    multipliers = warm_start * live[:, None, :]
    theta = (LOWER + UPPER) / 2.0
    delta = (UPPER - LOWER) / 2.0
    sigma = theta / delta
    rho = 1.0 / sigma
    update = jnp.zeros_like(multipliers)
    residual = jnp.zeros_like(multipliers)
    amplitudes = jnp.zeros((load.shape[1], NC), jnp.float32)
    for step in range(ITERS):
        unprojected = (load - apply_dual(multipliers, schur)) * live[:, None, :]
        coefficients = jnp.einsum('skh,sch->kc', unprojected, modes, precision=lax.Precision.HIGHEST)
        amplitudes = coarse_solve(factor, coefficients)
        residual = unprojected - jnp.einsum('kc,sch->skh', amplitudes, modes, precision=lax.Precision.HIGHEST)
        if step == 0:
            update = residual / theta
        else:
            rho_new = 1.0 / (2.0 * sigma - rho)
            update = rho_new * rho * update + 2.0 * rho_new / delta * residual
            rho = rho_new
        multipliers = multipliers + update
        multipliers = jnp.where(contact, jnp.maximum(multipliers, 0.0), multipliers)
    return (multipliers, residual, amplitudes)
```

```python
import functools
import math

import jax
import jax.numpy as jnp
from jax import lax
from jax.experimental import pallas as pl
from jax.experimental.pallas import tpu as pltpu
from jax.sharding import PartitionSpec as P

BLK = 128
ITERS = 3
LOWER = 0.1
UPPER = 8.0
THETA = (LOWER + UPPER) / 2.0
DELTA = (UPPER - LOWER) / 2.0
SIGMA = THETA / DELTA

AXES = ("group", "dev")
LANES = 128
ROWS = 8
CHUNK = 128
F32 = jnp.float32
BF16 = jnp.bfloat16
HIGHEST = lax.Precision.HIGHEST
VMEM = pl.BlockSpec(memory_space=pltpu.VMEM)
SMEM = pl.BlockSpec(memory_space=pltpu.SMEM)
ANY = pl.BlockSpec(memory_space=pl.ANY)


def split(x):
    high = x.astype(BF16)
    return high, (x - high.astype(F32)).astype(BF16)


def dot(a, b):
    return jnp.dot(a, b, preferred_element_type=F32)


def product(x, high, low):
    cases = x.shape[0]
    x_high, x_low = split(x)
    both = dot(jnp.concatenate([x_high, x_low], axis=0), high)
    return both[:cases] + (both[cases:] + dot(x_high, low))


def position():
    me = lax.axis_index("group") * lax.axis_size("dev") + lax.axis_index("dev")
    return me, lax.axis_size("group") * lax.axis_size("dev")


def pack_kernel(count_ref, from_ref, warm_ref, modes_ref, out_ref):
    cases, width = warm_ref.shape
    terms = modes_ref.shape[0]
    dofs = lax.broadcasted_iota(jnp.int32, (1, width), 1)
    alive = dofs < count_ref[0] * BLK
    live = alive.astype(F32)
    contact = (alive & (dofs >= from_ref[0])).astype(F32)
    out_ref[:cases, :] = warm_ref[...] * live
    out_ref[cases:, :] = jnp.zeros((2 * ROWS, width), F32)
    out_ref[cases : cases + terms, :] = modes_ref[...] * live
    out_ref[cases + ROWS : cases + ROWS + 1, :] = live
    out_ref[cases + ROWS + 1 : cases + ROWS + 2, :] = contact


def first_kernel(terms, schur_ref, msg_ref, high_ref, low_ref, own_ref, gram_ref, raw, acc, wide, sems):
    order = schur_ref.shape[0]
    cases = own_ref.shape[0]
    chunks = order // CHUNK
    half = chunks // 2
    sequence = list(range(half, chunks)) + list(range(half))

    def copy(c):
        rows = pl.ds(c * CHUNK, CHUNK)
        return pltpu.make_async_copy(schur_ref.at[rows, :], raw.at[rows, :], sems.at[c])

    for c in sequence:
        copy(c).start()
    modes = msg_ref[cases : cases + ROWS, :]
    wide[...] = jnp.zeros_like(wide)
    wide[:, :ROWS] = lax.dot_general(
        modes, modes, (((1,), (1,)), ((), ())), precision=HIGHEST, preferred_element_type=F32
    )
    row = wide[0:1, :]
    for c in range(1, terms):
        row = row + pltpu.roll(wide[c : c + 1, :], ROWS * c, 1)
    gram_ref[...] = row
    for n, c in enumerate(sequence):
        copy(c).wait()
        rows = pl.ds(c * CHUNK, CHUNK)
        high, low = split(raw[rows, :])
        high_ref[rows, :] = high
        low_ref[rows, :] = low
        if n < half:
            part = product(msg_ref[:cases, n * CHUNK : (n + 1) * CHUNK], high, low)
            if n == 0:
                acc[...] = part
            else:
                acc[...] += part
    own_ref[...] = acc[...]


def send(even, left_half, right_half, near_ref, far_ref):
    near_ref[...] = jnp.where(even, right_half, left_half)
    far_ref[...] = jnp.where(even, left_half, right_half)


def pay(terms, modes2, z2, gram_row, pay_ref):
    cases = z2.shape[0]
    per_row = LANES // cases
    coef = lax.dot_general(
        modes2, z2, (((1,), (1,)), ((), ())), precision=HIGHEST, preferred_element_type=F32
    )
    used = terms // per_row
    parts = [coef[p * used : (p + 1) * used, :] for p in range(per_row)]
    block = jnp.concatenate(parts, axis=1)
    slots = pay_ref.shape[0]
    pay_ref[:, :used, :] = jnp.broadcast_to(block[None], (slots, used, LANES))
    pay_ref[:, used : used + 1, :] = jnp.broadcast_to(gram_row[None], (slots, 1, LANES))


def second_kernel(
    terms, high_ref, low_ref, own_ref, halo_ref, msg_ref, load_ref, gram_ref,
    near_ref, far_ref, pay_ref, mult_ref, side_ref,
):
    cases, width = load_ref.shape
    me, _ = position()
    halo = jnp.where(me > 0, halo_ref[...], 0.0)
    left = halo[:cases]
    y = own_ref[...] - product(left, high_ref[:width, :], low_ref[:width, :])
    y_left = y[:, :width]
    rest = load_ref[...] - y[:, width:]
    side = jnp.concatenate([halo[cases:], msg_ref[cases:, :]], axis=1)
    send(me % 2 == 0, y_left, rest, near_ref, far_ref)
    pay(terms, side[:ROWS], jnp.concatenate([y_left, rest], axis=1), gram_ref[...], pay_ref)
    mult_ref[...] = jnp.concatenate([left, msg_ref[:cases, :]], axis=1)
    side_ref[...] = side


def factor_rows(row, terms):
    def entry(c, e):
        lane = ROWS * c + e
        return jnp.broadcast_to(row[:, lane : lane + 1], (1, LANES))

    lower = {}
    inverse = []
    for j in range(terms):
        pivot = entry(j, j)
        for k in range(j):
            pivot = pivot - lower[j, k] * lower[j, k]
        root = jnp.sqrt(pivot)
        inverse.append(1.0 / root)
        for i in range(j + 1, terms):
            value = entry(i, j)
            for k in range(j):
                value = value - lower[i, k] * lower[j, k]
            lower[i, j] = value * inverse[j]
    return lower, inverse


def store_factor(lower, inverse, fac_ref):
    terms = len(inverse)
    n = 0
    for j in range(terms):
        fac_ref[n : n + 1, :] = inverse[j]
        n += 1
    for j in range(terms):
        for i in range(j + 1, terms):
            fac_ref[n : n + 1, :] = lower[i, j]
            n += 1


def load_factor(terms, fac_ref):
    inverse = [fac_ref[j : j + 1, :] for j in range(terms)]
    lower = {}
    n = terms
    for j in range(terms):
        for i in range(j + 1, terms):
            lower[i, j] = fac_ref[n : n + 1, :]
            n += 1
    return lower, inverse


def solve(total, lower, inverse, cases, amp_ref):
    terms = len(inverse)
    per_row = LANES // cases
    used = terms // per_row
    known = []
    for c in range(terms):
        row = total[c % used : c % used + 1, :]
        value = row if c < used else pltpu.roll(row, LANES - (c // used) * cases, 1)
        for k in range(c):
            value = value - lower[c, k] * known[k]
        known.append(value * inverse[c])
    for c in reversed(range(terms)):
        value = known[c]
        for k in range(c + 1, terms):
            value = value - lower[k, c] * known[k]
        known[c] = value * inverse[c]
    amp_ref[...] = jnp.zeros_like(amp_ref)
    for c in range(terms):
        amp_ref[c : c + 1, :] = known[c]
    return amp_ref[...][:, :cases]


def chebyshev(residual, update, rhos):
    rho, rho_new = rhos
    if rho is None:
        return residual / THETA
    return rho_new * rho * update + 2.0 * rho_new / DELTA * residual


def project(amp, modes):
    return lax.dot_general(
        amp, modes, (((0,), (0,)), ((), ())), precision=HIGHEST, preferred_element_type=F32
    )


def middle_kernel(
    terms, first, rhos, sum_ref, near_ref, far_ref, near_in, far_in, mult_ref, side_ref, load_ref,
    high_ref, low_ref, *rest,
):
    if first:
        near_out, far_out, pay_ref, mult_out, upd_out, fac_out, amp_ref = rest
    else:
        upd_ref, fac_ref, near_out, far_out, pay_ref, mult_out, upd_out, amp_ref = rest
    cases, width = load_ref.shape
    me, devices = position()
    even = me % 2 == 0
    total = jnp.sum(sum_ref[...], axis=0)
    if first:
        used = total.shape[0] - 1
        lower, inverse = factor_rows(total[used : used + 1, :], terms)
        store_factor(lower, inverse, fac_out)
    else:
        lower, inverse = load_factor(terms, fac_ref)
    amp = solve(total, lower, inverse, cases, amp_ref)
    near = near_ref[...] + near_in[...]
    far = far_ref[...] + jnp.where((me == devices - 1), 0.0, far_in[...])
    live = side_ref[ROWS : ROWS + 1, :]
    contact = side_ref[ROWS + 1 : ROWS + 2, :] > 0.0
    modes = side_ref[:ROWS, :]
    open_part = jnp.concatenate([jnp.where(even, far, near), jnp.where(even, near, far)], axis=1)
    open_part = jnp.where(live > 0.0, open_part, 0.0)
    residual = open_part - project(amp, modes)
    update = chebyshev(residual, None if first else upd_ref[...], rhos)
    mult = mult_ref[...] + update
    mult = jnp.where(contact, jnp.maximum(mult, 0.0), mult)
    mult_out[...] = mult
    upd_out[...] = update
    y = product(jnp.concatenate([-mult[:, :width], mult[:, width:]], axis=1), high_ref[...], low_ref[...])
    y_left = y[:, :width]
    rest_part = load_ref[...] - y[:, width:]
    send(even, y_left, rest_part, near_out, far_out)
    pay(terms, modes, jnp.concatenate([y_left, rest_part], axis=1), jnp.zeros((1, LANES), F32), pay_ref)


def last_kernel(
    terms, rhos, sum_ref, near_ref, far_ref, near_in, far_in, mult_ref, side_ref, upd_ref, fac_ref,
    mult_out, res_out, amp_out, amp_ref,
):
    cases, width = mult_out.shape
    me, devices = position()
    even = me % 2 == 0
    total = jnp.sum(sum_ref[...], axis=0)
    lower, inverse = load_factor(terms, fac_ref)
    amp = solve(total, lower, inverse, cases, amp_ref)
    near = near_ref[...] + near_in[...]
    far = far_ref[...] + jnp.where((me == devices - 1), 0.0, far_in[...])
    live = side_ref[ROWS : ROWS + 1, width:]
    contact = side_ref[ROWS + 1 : ROWS + 2, width:] > 0.0
    open_part = jnp.where(live > 0.0, jnp.where(even, near, far), 0.0)
    residual = open_part - project(amp, side_ref[:ROWS, width:])
    update = chebyshev(residual, upd_ref[:, width:], rhos)
    mult = mult_ref[:, width:] + update
    mult_out[...] = jnp.where(contact, jnp.maximum(mult, 0.0), mult)
    res_out[...] = residual
    amp_out[...] = jnp.transpose(amp_ref[...])[:cases, :terms]


def shaped(*shapes):
    return [jax.ShapeDtypeStruct(s, d) for s, d in shapes]


def params(megabytes):
    return pltpu.CompilerParams(vmem_limit_bytes=megabytes << 20)


def shards(schur, coarse_modes, load, warm_start, active_blocks, contact_from):
    _, cases, width = load.shape
    order = schur.shape[1]
    terms = coarse_modes.shape[1]
    devices = lax.axis_size("group") * lax.axis_size("dev")
    slot = terms // (LANES // cases) + 1
    ring = [(i, (i + 1) % devices) for i in range(devices)]
    near_pairs = [(i, i ^ 1) for i in range(devices)]
    far_pairs = [(i, (i + (1 if i % 2 else devices - 1)) % devices) for i in range(devices)]

    rhos = [(None, None)]
    rho = 1.0 / SIGMA
    for _ in range(1, ITERS):
        rho_new = 1.0 / (2.0 * SIGMA - rho)
        rhos.append((rho, rho_new))
        rho = rho_new

    msg = pl.pallas_call(
        pack_kernel,
        out_shape=jax.ShapeDtypeStruct((cases + 2 * ROWS, width), F32),
        in_specs=[SMEM, SMEM, VMEM, VMEM],
        out_specs=VMEM,
        compiler_params=params(4),
        name="pack",
    )(active_blocks, contact_from, warm_start[0], coarse_modes[0])
    halo = lax.ppermute(msg, AXES, ring)
    high, low, own, gram_row = pl.pallas_call(
        functools.partial(first_kernel, terms),
        out_shape=shaped(
            ((order, order), BF16), ((order, order), BF16), ((cases, order), F32), ((1, LANES), F32)
        ),
        in_specs=[ANY, VMEM],
        out_specs=[VMEM] * 4,
        scratch_shapes=[
            pltpu.VMEM((order, order), F32),
            pltpu.VMEM((cases, order), F32),
            pltpu.VMEM((ROWS, LANES), F32),
            pltpu.SemaphoreType.DMA((order // CHUNK,)),
        ],
        compiler_params=params(16),
        cost_estimate=pl.CostEstimate(
            flops=4 * cases * order * order, bytes_accessed=8 * order * order, transcendentals=0
        ),
        name="first",
    )(schur[0], msg)

    half = ((cases, width), F32)
    full = ((cases, order), F32)
    payload = ((devices, slot, LANES), F32)
    rows = ((math.ceil(terms * (terms + 1) // 2 / ROWS) * ROWS, LANES), F32)
    near, far, pay_out, mult, side = pl.pallas_call(
        functools.partial(second_kernel, terms),
        out_shape=shaped(half, half, payload, full, ((2 * ROWS, order), F32)),
        in_specs=[VMEM] * 7,
        out_specs=[VMEM] * 5,
        compiler_params=params(8),
        name="second",
    )(high, low, own, halo, msg, load[0], gram_row)

    update = factor = None
    amp_scratch = [pltpu.VMEM((ROWS, LANES), F32)]
    for step in range(ITERS):
        far_in = lax.ppermute(far, AXES, far_pairs)
        near_in = lax.ppermute(near, AXES, near_pairs)
        gathered = lax.all_to_all(pay_out, AXES, 0, 0)
        first = step == 0
        if step < ITERS - 1:
            inputs = [gathered, near, far, near_in, far_in, mult, side, load[0], high, low]
            outputs = [half, half, payload, full, full]
            if first:
                outputs.append(rows)
            else:
                inputs += [update, factor]
            out = pl.pallas_call(
                functools.partial(middle_kernel, terms, first, rhos[step]),
                out_shape=shaped(*outputs),
                in_specs=[VMEM] * len(inputs),
                out_specs=[VMEM] * len(outputs),
                scratch_shapes=amp_scratch,
                compiler_params=params(12),
            )(*inputs)
            near, far, pay_out, mult, update = out[:5]
            if first:
                factor = out[5]
        else:
            inputs = [gathered, near, far, near_in, far_in, mult, side, update, factor]
            mult, residual, amplitudes = pl.pallas_call(
                functools.partial(last_kernel, terms, rhos[step]),
                out_shape=shaped(half, half, ((cases, terms), F32)),
                in_specs=[VMEM] * len(inputs),
                out_specs=[VMEM] * 3,
                scratch_shapes=amp_scratch,
                compiler_params=params(8),
                name="last",
            )(*inputs)
    return mult[None], residual[None], amplitudes


def solution(mesh):
    placed = (
        P(AXES, None, None),
        P(AXES, None, None),
        P(AXES, None, None),
        P(AXES, None, None),
        P(AXES),
        P(AXES),
    )
    return jax.shard_map(
        shards,
        mesh=mesh,
        in_specs=placed,
        out_specs=(P(AXES, None, None), P(AXES, None, None), P()),
        check_vma=False,
    )
```

```python
import functools
import math

import jax
import jax.numpy as jnp
from jax import lax
from jax.experimental import pallas as pl
from jax.experimental.pallas import tpu as pltpu
from jax.sharding import PartitionSpec as P

BLK = 128
ITERS = 3
LOWER = 0.1
UPPER = 8.0
THETA = (LOWER + UPPER) / 2.0
DELTA = (UPPER - LOWER) / 2.0
SIGMA = THETA / DELTA

AXES = ("group", "dev")
LANES = 128
ROWS = 8
CHUNK = 128
F32 = jnp.float32
BF16 = jnp.bfloat16
HIGHEST = lax.Precision.HIGHEST
VMEM = pl.BlockSpec(memory_space=pltpu.VMEM)
SMEM = pl.BlockSpec(memory_space=pltpu.SMEM)
ANY = pl.BlockSpec(memory_space=pl.ANY)


def split(x):
    high = x.astype(BF16)
    return high, (x - high.astype(F32)).astype(BF16)


def split3(x):
    high = x.astype(BF16)
    rest = x - high.astype(F32)
    middle = rest.astype(BF16)
    return high, middle, (rest - middle.astype(F32)).astype(BF16)


def dot(a, b):
    return jnp.dot(a, b, preferred_element_type=F32)


def product(x, high, low):
    cases = x.shape[0]
    x_high, x_low = split(x)
    both = dot(jnp.concatenate([x_high, x_low], axis=0), high)
    return both[:cases] + (both[cases:] + dot(x_high, low))


def wide_product(x, high_ref, low_ref, start):
    cases, depth = x.shape
    x_high, x_low = split(x)
    both = jnp.concatenate([x_high, x_low], axis=0)
    out = []
    for j in range(0, high_ref.shape[0], 2):
        high = jnp.concatenate([high_ref[j + p, start : start + depth, :] for p in range(2)], axis=1)
        low = jnp.concatenate([low_ref[j + p, start : start + depth, :] for p in range(2)], axis=1)
        first = dot(both, high)
        out.append(first[:cases] + (first[cases:] + dot(x_high, low)))
    return jnp.concatenate(out, axis=1)


def position():
    me = lax.axis_index("group") * lax.axis_size("dev") + lax.axis_index("dev")
    return me, lax.axis_size("group") * lax.axis_size("dev")


def pack_kernel(count_ref, from_ref, warm_ref, modes_ref, out_ref):
    cases, width = warm_ref.shape
    terms = modes_ref.shape[0]
    spare = out_ref.shape[0] - cases - terms
    dofs = lax.broadcasted_iota(jnp.int32, (1, width), 1)
    alive = dofs < count_ref[0] * BLK
    live = alive.astype(F32)
    contact = (alive & (dofs >= from_ref[0])).astype(F32)
    out_ref[:cases, :] = warm_ref[...] * live
    for c in range(terms):
        out_ref[cases + c : cases + c + 1, :] = modes_ref[c] * live
    if spare > 2:
        out_ref[cases + terms :, :] = jnp.zeros((spare, width), F32)
    out_ref[-2:-1, :] = live
    out_ref[-1:, :] = contact


def first_kernel(terms, schur_ref, msg_ref, high_ref, low_ref, own_ref, gram_ref, raw, acc, wide, sems):
    order = schur_ref.shape[0]
    cases = own_ref.shape[0]
    chunks = order // CHUNK
    half = chunks // 2
    sequence = list(range(half, chunks)) + list(range(half))

    def copy(c):
        rows = pl.ds(c * CHUNK, CHUNK)
        return pltpu.make_async_copy(schur_ref.at[rows, :], raw.at[rows, :], sems.at[c])

    for c in sequence:
        copy(c).start()
    modes = msg_ref[cases : cases + ROWS, :]
    modes = jnp.where(lax.broadcasted_iota(jnp.int32, modes.shape, 0) < terms, modes, 0.0)
    wide[...] = jnp.zeros_like(wide)
    wide[:, :ROWS] = lax.dot_general(
        modes, modes, (((1,), (1,)), ((), ())), precision=HIGHEST, preferred_element_type=F32
    )
    row = wide[0:1, :]
    for c in range(1, terms):
        row = row + pltpu.roll(wide[c : c + 1, :], ROWS * c, 1)
    gram_ref[...] = row
    for n, c in enumerate(sequence):
        copy(c).wait()
        rows = pl.ds(c * CHUNK, CHUNK)
        high, low = split(raw[rows, :])
        for j in range(order // LANES):
            lanes = slice(j * LANES, (j + 1) * LANES)
            high_ref[j, c * CHUNK : (c + 1) * CHUNK, :] = high[:, lanes]
            low_ref[j, c * CHUNK : (c + 1) * CHUNK, :] = low[:, lanes]
        if n < half:
            part = product(msg_ref[:cases, n * CHUNK : (n + 1) * CHUNK], high, low)
            if n == 0:
                acc[...] = part
            else:
                acc[...] += part
    own_ref[...] = acc[...]


def send(even, left_half, right_half, near_ref, far_ref):
    near_ref[...] = jnp.where(even, right_half, left_half)
    far_ref[...] = jnp.where(even, left_half, right_half)


def pay(terms, pieces, z2, gram_row, pay_ref):
    cases = z2.shape[0]
    per_row = LANES // cases
    across = (((1,), (1,)), ((), ()))
    z_high, z_low = split(z2)
    top = lax.dot_general(pieces, z_high, across, preferred_element_type=F32)
    low = lax.dot_general(pieces, z_low, across, preferred_element_type=F32)
    coef = top[:ROWS] + ((top[ROWS : 2 * ROWS] + low[:ROWS]) + (top[2 * ROWS : 3 * ROWS] + low[ROWS : 2 * ROWS]))
    used = terms // per_row
    parts = [coef[p * used : (p + 1) * used, :] for p in range(per_row)]
    block = jnp.concatenate(parts, axis=1)
    slots = pay_ref.shape[0]
    pay_ref[:, :used, :] = jnp.broadcast_to(block[None], (slots, used, LANES))
    pay_ref[:, used : used + 1, :] = jnp.broadcast_to(gram_row[None], (slots, 1, LANES))


def second_kernel(
    terms, high_ref, low_ref, own_ref, halo_ref, msg_ref, load_ref, gram_ref,
    near_ref, far_ref, pay_ref, mult_ref, mask_ref, pieces_ref,
):
    cases, width = load_ref.shape
    me, _ = position()
    halo = jnp.where(me > 0, halo_ref[...], 0.0)
    left = halo[:cases]
    y = own_ref[...] - wide_product(left, high_ref, low_ref, 0)
    y_left = y[:, :width]
    rest = load_ref[...] - y[:, width:]
    tail = halo_ref.shape[0] - 2
    mask_ref[0:2, :] = jnp.concatenate([halo[tail:], msg_ref[tail:, :]], axis=1)
    modes = jnp.concatenate([halo[cases : cases + ROWS], msg_ref[cases : cases + ROWS, :]], axis=1)
    modes = jnp.where(lax.broadcasted_iota(jnp.int32, modes.shape, 0) < terms, modes, 0.0)
    pieces = jnp.concatenate(split3(modes), axis=0)
    pieces_ref[...] = pieces
    send(me % 2 == 0, y_left, rest, near_ref, far_ref)
    pay(terms, pieces, jnp.concatenate([y_left, rest], axis=1), gram_ref[...], pay_ref)
    mult_ref[...] = jnp.concatenate([left, msg_ref[:cases, :]], axis=1)


def factor_rows(row, terms):
    def entry(c, e):
        lane = ROWS * c + e
        return jnp.broadcast_to(row[:, lane : lane + 1], (1, LANES))

    lower = {}
    inverse = []
    for j in range(terms):
        pivot = entry(j, j)
        for k in range(j):
            pivot = pivot - lower[j, k] * lower[j, k]
        root = jnp.sqrt(pivot)
        inverse.append(1.0 / root)
        for i in range(j + 1, terms):
            value = entry(i, j)
            for k in range(j):
                value = value - lower[i, k] * lower[j, k]
            lower[i, j] = value * inverse[j]
    return lower, inverse


def store_factor(lower, inverse, fac_ref):
    terms = len(inverse)
    n = 0
    for j in range(terms):
        fac_ref[n : n + 1, :] = inverse[j]
        n += 1
    for j in range(terms):
        for i in range(j + 1, terms):
            fac_ref[n : n + 1, :] = lower[i, j]
            n += 1


def load_factor(terms, fac_ref):
    inverse = [fac_ref[j : j + 1, :] for j in range(terms)]
    lower = {}
    n = terms
    for j in range(terms):
        for i in range(j + 1, terms):
            lower[i, j] = fac_ref[n : n + 1, :]
            n += 1
    return lower, inverse


def solve(total, lower, inverse, cases, amp_ref):
    terms = len(inverse)
    per_row = LANES // cases
    used = terms // per_row
    known = []
    for c in range(terms):
        row = total[c % used : c % used + 1, :]
        value = row if c < used else pltpu.roll(row, LANES - (c // used) * cases, 1)
        for k in range(c):
            value = value - lower[c, k] * known[k]
        known.append(value * inverse[c])
    for c in reversed(range(terms)):
        value = known[c]
        for k in range(c + 1, terms):
            value = value - lower[k, c] * known[k]
        known[c] = value * inverse[c]
    amp_ref[...] = jnp.zeros_like(amp_ref)
    for c in range(terms):
        amp_ref[c : c + 1, :] = known[c]
    return amp_ref[...]


def chebyshev(residual, update, rhos):
    rho, rho_new = rhos
    if rho is None:
        return residual / THETA
    return rho_new * rho * update + 2.0 * rho_new / DELTA * residual


def project(amp, pieces, cases):
    one, two, three = (p.astype(F32) for p in split3(amp))
    left = jnp.transpose(jnp.concatenate([one, two, three, one, two, one], axis=0))[:cases]
    m = [pieces[p * ROWS : (p + 1) * ROWS] for p in range(3)]
    right = jnp.concatenate([m[0], m[0], m[0], m[1], m[1], m[2]], axis=0)
    return dot(left.astype(BF16), right)


def middle_kernel(
    terms, first, rhos, sum_ref, near_ref, far_ref, near_in, far_in, mult_ref, mask_ref, pieces_ref, load_ref,
    high_ref, low_ref, *rest,
):
    if first:
        near_out, far_out, pay_ref, mult_out, upd_out, fac_out, amp_ref = rest
    else:
        upd_ref, fac_ref, near_out, far_out, pay_ref, mult_out, upd_out, amp_ref = rest
    cases, width = load_ref.shape
    me, devices = position()
    even = me % 2 == 0
    total = jnp.sum(sum_ref[...], axis=0)
    if first:
        used = total.shape[0] - 1
        lower, inverse = factor_rows(total[used : used + 1, :], terms)
        store_factor(lower, inverse, fac_out)
    else:
        lower, inverse = load_factor(terms, fac_ref)
    amp = solve(total, lower, inverse, cases, amp_ref)
    near = near_ref[...] + near_in[...]
    far = far_ref[...] + jnp.where((me == devices - 1), 0.0, far_in[...])
    live = mask_ref[0:1, :]
    contact = mask_ref[1:2, :] > 0.0
    pieces = pieces_ref[...]
    open_part = jnp.concatenate([jnp.where(even, far, near), jnp.where(even, near, far)], axis=1)
    open_part = jnp.where(live > 0.0, open_part, 0.0)
    residual = open_part - project(amp, pieces, cases)
    update = chebyshev(residual, None if first else upd_ref[...], rhos)
    mult = mult_ref[...] + update
    mult = jnp.where(contact, jnp.maximum(mult, 0.0), mult)
    mult_out[...] = mult
    upd_out[...] = update
    y = wide_product(jnp.concatenate([-mult[:, :width], mult[:, width:]], axis=1), high_ref, low_ref, 0)
    y_left = y[:, :width]
    rest_part = load_ref[...] - y[:, width:]
    send(even, y_left, rest_part, near_out, far_out)
    pay(terms, pieces, jnp.concatenate([y_left, rest_part], axis=1), jnp.zeros((1, LANES), F32), pay_ref)


def last_kernel(
    terms, rhos, sum_ref, near_ref, far_ref, near_in, far_in, mult_ref, mask_ref, pieces_ref, upd_ref, fac_ref,
    mult_out, res_out, amp_out, amp_ref,
):
    cases, width = mult_out.shape
    me, devices = position()
    even = me % 2 == 0
    total = jnp.sum(sum_ref[...], axis=0)
    lower, inverse = load_factor(terms, fac_ref)
    amp = solve(total, lower, inverse, cases, amp_ref)
    near = near_ref[...] + near_in[...]
    far = far_ref[...] + jnp.where((me == devices - 1), 0.0, far_in[...])
    live = mask_ref[0:1, width:]
    contact = mask_ref[1:2, width:] > 0.0
    open_part = jnp.where(live > 0.0, jnp.where(even, near, far), 0.0)
    residual = open_part - project(amp, pieces_ref[:, width:], cases)
    update = chebyshev(residual, upd_ref[:, width:], rhos)
    mult = mult_ref[:, width:] + update
    mult_out[...] = jnp.where(contact, jnp.maximum(mult, 0.0), mult)
    res_out[...] = residual
    amp_out[...] = amp_ref[:terms, :cases]


def rows_of(count):
    return math.ceil(count / ROWS) * ROWS


def shaped(*shapes):
    return [jax.ShapeDtypeStruct(s, d) for s, d in shapes]


def params(megabytes):
    return pltpu.CompilerParams(vmem_limit_bytes=megabytes << 20)


def shards(schur, coarse_modes, load, warm_start, active_blocks, contact_from):
    _, cases, width = load.shape
    order = schur.shape[1]
    terms = coarse_modes.shape[1]
    devices = lax.axis_size("group") * lax.axis_size("dev")
    blocks = (order // LANES, order, LANES)
    slot = terms // (LANES // cases) + 1
    ring = [(i, (i + 1) % devices) for i in range(devices)]
    near_pairs = [(i, i ^ 1) for i in range(devices)]
    far_pairs = [(i, (i + (1 if i % 2 else devices - 1)) % devices) for i in range(devices)]

    rhos = [(None, None)]
    rho = 1.0 / SIGMA
    for _ in range(1, ITERS):
        rho_new = 1.0 / (2.0 * SIGMA - rho)
        rhos.append((rho, rho_new))
        rho = rho_new

    msg = pl.pallas_call(
        pack_kernel,
        out_shape=jax.ShapeDtypeStruct((rows_of(cases + terms + 2), width), F32),
        in_specs=[SMEM, SMEM, VMEM, VMEM],
        out_specs=VMEM,
        compiler_params=params(4),
        name="pack",
    )(active_blocks, contact_from, warm_start[0], jnp.transpose(coarse_modes, (1, 0, 2)))
    halo = lax.ppermute(msg, AXES, ring)
    high, low, own, gram_row = pl.pallas_call(
        functools.partial(first_kernel, terms),
        out_shape=shaped(
            (blocks, BF16), (blocks, BF16), ((cases, order), F32), ((1, LANES), F32)
        ),
        in_specs=[ANY, VMEM],
        out_specs=[VMEM] * 4,
        scratch_shapes=[
            pltpu.VMEM((order, order), F32),
            pltpu.VMEM((cases, order), F32),
            pltpu.VMEM((ROWS, LANES), F32),
            pltpu.SemaphoreType.DMA((order // CHUNK,)),
        ],
        compiler_params=params(16),
        cost_estimate=pl.CostEstimate(
            flops=4 * cases * order * order, bytes_accessed=8 * order * order, transcendentals=0
        ),
        name="first",
    )(schur[0], msg)

    half = ((cases, width), F32)
    full = ((cases, order), F32)
    payload = ((devices, slot, LANES), F32)
    rows = ((rows_of(terms * (terms + 1) // 2), LANES), F32)
    near, far, pay_out, mult, masks, pieces = pl.pallas_call(
        functools.partial(second_kernel, terms),
        out_shape=shaped(half, half, payload, full, ((2, order), F32), ((3 * ROWS, order), BF16)),
        in_specs=[VMEM] * 7,
        out_specs=[VMEM] * 6,
        compiler_params=params(8),
        name="second",
    )(high, low, own, halo, msg, load[0], gram_row)

    update = factor = None
    amp_scratch = [pltpu.VMEM((ROWS, LANES), F32)]
    for step in range(ITERS):
        far_in = lax.ppermute(far, AXES, far_pairs)
        near_in = lax.ppermute(near, AXES, near_pairs)
        gathered = lax.all_to_all(pay_out, AXES, 0, 0)
        first = step == 0
        if step < ITERS - 1:
            inputs = [gathered, near, far, near_in, far_in, mult, masks, pieces, load[0], high, low]
            outputs = [half, half, payload, full, full]
            if first:
                outputs.append(rows)
            else:
                inputs += [update, factor]
            out = pl.pallas_call(
                functools.partial(middle_kernel, terms, first, rhos[step]),
                out_shape=shaped(*outputs),
                in_specs=[VMEM] * len(inputs),
                out_specs=[VMEM] * len(outputs),
                scratch_shapes=amp_scratch,
                compiler_params=params(12),
            )(*inputs)
            near, far, pay_out, mult, update = out[:5]
            if first:
                factor = out[5]
        else:
            inputs = [gathered, near, far, near_in, far_in, mult, masks, pieces, update, factor]
            mult, residual, amplitudes = pl.pallas_call(
                functools.partial(last_kernel, terms, rhos[step]),
                out_shape=shaped(half, half, ((terms, cases), F32)),
                in_specs=[VMEM] * len(inputs),
                out_specs=[VMEM] * 3,
                scratch_shapes=amp_scratch,
                compiler_params=params(8),
                name="last",
            )(*inputs)
    return mult[None], residual[None], amplitudes.T


def solution(mesh):
    placed = (
        P(AXES, None, None),
        P(AXES, None, None),
        P(AXES, None, None),
        P(AXES, None, None),
        P(AXES),
        P(AXES),
    )
    return jax.shard_map(
        shards,
        mesh=mesh,
        in_specs=placed,
        out_specs=(P(AXES, None, None), P(AXES, None, None), P()),
        check_vma=False,
    )
```

```python
import functools
import math

import jax
import jax.numpy as jnp
from jax import lax
from jax.experimental import pallas as pl
from jax.experimental.pallas import tpu as pltpu
from jax.sharding import PartitionSpec as P

BLK = 128
ITERS = 3
LOWER = 0.1
UPPER = 8.0
THETA = (LOWER + UPPER) / 2.0
DELTA = (UPPER - LOWER) / 2.0
SIGMA = THETA / DELTA

AXES = ("group", "dev")
LANES = 128
ROWS = 8
CHUNK = 128
F32 = jnp.float32
BF16 = jnp.bfloat16
HIGHEST = lax.Precision.HIGHEST
VMEM = pl.BlockSpec(memory_space=pltpu.VMEM)
SMEM = pl.BlockSpec(memory_space=pltpu.SMEM)
HBM = pl.BlockSpec(memory_space=pltpu.HBM)


def split(x):
    high = x.astype(BF16)
    return high, (x - high.astype(F32)).astype(BF16)


def split3(x):
    high = x.astype(BF16)
    rest = x - high.astype(F32)
    middle = rest.astype(BF16)
    return high, middle, (rest - middle.astype(F32)).astype(BF16)


def dot(a, b):
    return jnp.dot(a, b, preferred_element_type=F32)


def product(x, high, low):
    cases = x.shape[0]
    x_high, x_low = split(x)
    both = dot(jnp.concatenate([x_high, x_low], axis=0), high)
    return both[:cases] + (both[cases:] + dot(x_high, low))


def wide_product(x, high_ref, low_ref, start):
    cases, depth = x.shape
    x_high, x_low = split(x)
    both = jnp.concatenate([x_high, x_low], axis=0)
    out = []
    for j in range(0, high_ref.shape[0], 2):
        high = jnp.concatenate([high_ref[j + p, start : start + depth, :] for p in range(2)], axis=1)
        low = jnp.concatenate([low_ref[j + p, start : start + depth, :] for p in range(2)], axis=1)
        first = dot(both, high)
        out.append(first[:cases] + (first[cases:] + dot(x_high, low)))
    return jnp.concatenate(out, axis=1)


def position():
    me = lax.axis_index("group") * lax.axis_size("dev") + lax.axis_index("dev")
    return me, lax.axis_size("group") * lax.axis_size("dev")


def pack_kernel(count_ref, from_ref, warm_hbm, modes_hbm, out_ref, warm_ref, modes_ref, sems):
    copies = [
        pltpu.make_async_copy(source, target, sems.at[n])
        for n, (source, target) in enumerate(((warm_hbm, warm_ref), (modes_hbm, modes_ref)))
    ]
    for copy in copies:
        copy.start()
    cases, width = warm_ref.shape
    terms = modes_ref.shape[0]
    spare = out_ref.shape[0] - cases - terms
    dofs = lax.broadcasted_iota(jnp.int32, (1, width), 1)
    alive = dofs < count_ref[0] * BLK
    live = alive.astype(F32)
    contact = (alive & (dofs >= from_ref[0])).astype(F32)
    for copy in copies:
        copy.wait()
    out_ref[:cases, :] = warm_ref[...] * live
    for c in range(terms):
        out_ref[cases + c : cases + c + 1, :] = modes_ref[c] * live
    if spare > 2:
        out_ref[cases + terms :, :] = jnp.zeros((spare, width), F32)
    out_ref[-2:-1, :] = live
    out_ref[-1:, :] = contact


def first_kernel(terms, schur_ref, msg_ref, high_ref, low_ref, own_ref, gram_ref, raw, acc, wide, sems):
    order = schur_ref.shape[0]
    cases = own_ref.shape[0]
    chunks = order // CHUNK
    half = chunks // 2
    sequence = list(range(half, chunks)) + list(range(half))

    def copy(c):
        rows = pl.ds(c * CHUNK, CHUNK)
        return pltpu.make_async_copy(schur_ref.at[rows, :], raw.at[rows, :], sems.at[c])

    for c in sequence:
        copy(c).start()
    modes = msg_ref[cases : cases + ROWS, :]
    modes = jnp.where(lax.broadcasted_iota(jnp.int32, modes.shape, 0) < terms, modes, 0.0)
    wide[...] = jnp.zeros_like(wide)
    wide[:, :ROWS] = lax.dot_general(
        modes, modes, (((1,), (1,)), ((), ())), precision=HIGHEST, preferred_element_type=F32
    )
    row = wide[0:1, :]
    for c in range(1, terms):
        row = row + pltpu.roll(wide[c : c + 1, :], ROWS * c, 1)
    gram_ref[...] = row
    for n, c in enumerate(sequence):
        copy(c).wait()
        rows = pl.ds(c * CHUNK, CHUNK)
        high, low = split(raw[rows, :])
        for j in range(order // LANES):
            lanes = slice(j * LANES, (j + 1) * LANES)
            high_ref[j, c * CHUNK : (c + 1) * CHUNK, :] = high[:, lanes]
            low_ref[j, c * CHUNK : (c + 1) * CHUNK, :] = low[:, lanes]
        if n < half:
            part = product(msg_ref[:cases, n * CHUNK : (n + 1) * CHUNK], high, low)
            if n == 0:
                acc[...] = part
            else:
                acc[...] += part
    own_ref[...] = acc[...]


def send(even, left_half, right_half, near_ref, far_ref):
    near_ref[...] = jnp.where(even, right_half, left_half)
    far_ref[...] = jnp.where(even, left_half, right_half)


def pay(terms, pieces, z2, gram_row, pay_ref):
    cases = z2.shape[0]
    per_row = LANES // cases
    across = (((1,), (1,)), ((), ()))
    z_high, z_low = split(z2)
    top = lax.dot_general(pieces, z_high, across, preferred_element_type=F32)
    low = lax.dot_general(pieces, z_low, across, preferred_element_type=F32)
    coef = top[:ROWS] + ((top[ROWS : 2 * ROWS] + low[:ROWS]) + (top[2 * ROWS : 3 * ROWS] + low[ROWS : 2 * ROWS]))
    used = terms // per_row
    parts = [coef[p * used : (p + 1) * used, :] for p in range(per_row)]
    block = jnp.concatenate(parts, axis=1)
    slots = pay_ref.shape[0]
    pay_ref[:, :used, :] = jnp.broadcast_to(block[None], (slots, used, LANES))
    pay_ref[:, used : used + 1, :] = jnp.broadcast_to(gram_row[None], (slots, 1, LANES))


def second_kernel(
    terms, high_ref, low_ref, own_ref, halo_ref, msg_ref, load_ref, gram_ref,
    near_ref, far_ref, pay_ref, mult_ref, mask_ref, pieces_ref,
):
    cases, width = load_ref.shape
    me, _ = position()
    halo = jnp.where(me > 0, halo_ref[...], 0.0)
    left = halo[:cases]
    y = own_ref[...] - wide_product(left, high_ref, low_ref, 0)
    y_left = y[:, :width]
    rest = load_ref[...] - y[:, width:]
    tail = halo_ref.shape[0] - 2
    mask_ref[0:2, :] = jnp.concatenate([halo[tail:], msg_ref[tail:, :]], axis=1)
    modes = jnp.concatenate([halo[cases : cases + ROWS], msg_ref[cases : cases + ROWS, :]], axis=1)
    modes = jnp.where(lax.broadcasted_iota(jnp.int32, modes.shape, 0) < terms, modes, 0.0)
    pieces = jnp.concatenate(split3(modes), axis=0)
    pieces_ref[...] = pieces
    send(me % 2 == 0, y_left, rest, near_ref, far_ref)
    pay(terms, pieces, jnp.concatenate([y_left, rest], axis=1), gram_ref[...], pay_ref)
    mult_ref[...] = jnp.concatenate([left, msg_ref[:cases, :]], axis=1)


def factor_rows(row, terms):
    def entry(c, e):
        lane = ROWS * c + e
        return jnp.broadcast_to(row[:, lane : lane + 1], (1, LANES))

    lower = {}
    inverse = []
    for j in range(terms):
        pivot = entry(j, j)
        for k in range(j):
            pivot = pivot - lower[j, k] * lower[j, k]
        root = jnp.sqrt(pivot)
        inverse.append(1.0 / root)
        for i in range(j + 1, terms):
            value = entry(i, j)
            for k in range(j):
                value = value - lower[i, k] * lower[j, k]
            lower[i, j] = value * inverse[j]
    return lower, inverse


def store_factor(lower, inverse, fac_ref):
    terms = len(inverse)
    n = 0
    for j in range(terms):
        fac_ref[n : n + 1, :] = inverse[j]
        n += 1
    for j in range(terms):
        for i in range(j + 1, terms):
            fac_ref[n : n + 1, :] = lower[i, j]
            n += 1


def load_factor(terms, fac_ref):
    inverse = [fac_ref[j : j + 1, :] for j in range(terms)]
    lower = {}
    n = terms
    for j in range(terms):
        for i in range(j + 1, terms):
            lower[i, j] = fac_ref[n : n + 1, :]
            n += 1
    return lower, inverse


def solve(total, lower, inverse, cases, amp_ref):
    terms = len(inverse)
    per_row = LANES // cases
    used = terms // per_row
    known = []
    for c in range(terms):
        row = total[c % used : c % used + 1, :]
        value = row if c < used else pltpu.roll(row, LANES - (c // used) * cases, 1)
        for k in range(c):
            value = value - lower[c, k] * known[k]
        known.append(value * inverse[c])
    for c in reversed(range(terms)):
        value = known[c]
        for k in range(c + 1, terms):
            value = value - lower[k, c] * known[k]
        known[c] = value * inverse[c]
    amp_ref[...] = jnp.zeros_like(amp_ref)
    for c in range(terms):
        amp_ref[c : c + 1, :] = known[c]
    return amp_ref[...]


def chebyshev(residual, update, rhos):
    rho, rho_new = rhos
    if rho is None:
        return residual / THETA
    return rho_new * rho * update + 2.0 * rho_new / DELTA * residual


def project(amp, pieces, cases):
    one, two, three = (p.astype(F32) for p in split3(amp))
    left = jnp.transpose(jnp.concatenate([one, two, three, one, two, one], axis=0))[:cases]
    m = [pieces[p * ROWS : (p + 1) * ROWS] for p in range(3)]
    right = jnp.concatenate([m[0], m[0], m[0], m[1], m[1], m[2]], axis=0)
    return dot(left.astype(BF16), right)


def middle_kernel(
    terms, first, rhos, sum_ref, near_ref, far_ref, near_in, far_in, mult_ref, mask_ref, pieces_ref, load_ref,
    high_ref, low_ref, *rest,
):
    if first:
        near_out, far_out, pay_ref, mult_out, upd_out, fac_out, amp_ref = rest
    else:
        upd_ref, fac_ref, near_out, far_out, pay_ref, mult_out, upd_out, amp_ref = rest
    cases, width = load_ref.shape
    me, devices = position()
    even = me % 2 == 0
    total = jnp.sum(sum_ref[...], axis=0)
    if first:
        used = total.shape[0] - 1
        lower, inverse = factor_rows(total[used : used + 1, :], terms)
        store_factor(lower, inverse, fac_out)
    else:
        lower, inverse = load_factor(terms, fac_ref)
    amp = solve(total, lower, inverse, cases, amp_ref)
    near = near_ref[...] + near_in[...]
    far = far_ref[...] + jnp.where((me == devices - 1), 0.0, far_in[...])
    live = mask_ref[0:1, :]
    contact = mask_ref[1:2, :] > 0.0
    pieces = pieces_ref[...]
    open_part = jnp.concatenate([jnp.where(even, far, near), jnp.where(even, near, far)], axis=1)
    open_part = jnp.where(live > 0.0, open_part, 0.0)
    residual = open_part - project(amp, pieces, cases)
    update = chebyshev(residual, None if first else upd_ref[...], rhos)
    mult = mult_ref[...] + update
    mult = jnp.where(contact, jnp.maximum(mult, 0.0), mult)
    mult_out[...] = mult
    upd_out[...] = update
    y = wide_product(jnp.concatenate([-mult[:, :width], mult[:, width:]], axis=1), high_ref, low_ref, 0)
    y_left = y[:, :width]
    rest_part = load_ref[...] - y[:, width:]
    send(even, y_left, rest_part, near_out, far_out)
    pay(terms, pieces, jnp.concatenate([y_left, rest_part], axis=1), jnp.zeros((1, LANES), F32), pay_ref)


def last_kernel(
    terms, rhos, sum_ref, near_ref, far_ref, near_in, far_in, mult_ref, mask_ref, pieces_ref, upd_ref, fac_ref,
    mult_out, res_out, amp_out, amp_ref,
):
    cases, width = mult_out.shape
    me, devices = position()
    even = me % 2 == 0
    total = jnp.sum(sum_ref[...], axis=0)
    lower, inverse = load_factor(terms, fac_ref)
    amp = solve(total, lower, inverse, cases, amp_ref)
    near = near_ref[...] + near_in[...]
    far = far_ref[...] + jnp.where((me == devices - 1), 0.0, far_in[...])
    live = mask_ref[0:1, width:]
    contact = mask_ref[1:2, width:] > 0.0
    open_part = jnp.where(live > 0.0, jnp.where(even, near, far), 0.0)
    residual = open_part - project(amp, pieces_ref[:, width:], cases)
    update = chebyshev(residual, upd_ref[:, width:], rhos)
    mult = mult_ref[:, width:] + update
    mult_out[...] = jnp.where(contact, jnp.maximum(mult, 0.0), mult)
    res_out[...] = residual
    amp_out[...] = amp_ref[:terms, :cases]


def rows_of(count):
    return math.ceil(count / ROWS) * ROWS


def shaped(*shapes):
    return [jax.ShapeDtypeStruct(s, d) for s, d in shapes]


def in_hbm(x):
    return pltpu.with_memory_space_constraint(x, pltpu.HBM)


def params(megabytes):
    return pltpu.CompilerParams(vmem_limit_bytes=megabytes << 20)


def shards(schur, coarse_modes, load, warm_start, active_blocks, contact_from):
    _, cases, width = load.shape
    order = schur.shape[1]
    terms = coarse_modes.shape[1]
    devices = lax.axis_size("group") * lax.axis_size("dev")
    blocks = (order // LANES, order, LANES)
    slot = terms // (LANES // cases) + 1
    ring = [(i, (i + 1) % devices) for i in range(devices)]
    near_pairs = [(i, i ^ 1) for i in range(devices)]
    far_pairs = [(i, (i + (1 if i % 2 else devices - 1)) % devices) for i in range(devices)]

    rhos = [(None, None)]
    rho = 1.0 / SIGMA
    for _ in range(1, ITERS):
        rho_new = 1.0 / (2.0 * SIGMA - rho)
        rhos.append((rho, rho_new))
        rho = rho_new

    msg = pl.pallas_call(
        pack_kernel,
        out_shape=jax.ShapeDtypeStruct((rows_of(cases + terms + 2), width), F32),
        in_specs=[SMEM, SMEM, HBM, HBM],
        out_specs=VMEM,
        scratch_shapes=[
            pltpu.VMEM((cases, width), F32),
            pltpu.VMEM((terms, 1, width), F32),
            pltpu.SemaphoreType.DMA((2,)),
        ],
        compiler_params=params(4),
        name="pack",
    )(active_blocks, contact_from, in_hbm(warm_start[0]), in_hbm(jnp.transpose(coarse_modes, (1, 0, 2))))
    halo = lax.ppermute(msg, AXES, ring)
    high, low, own, gram_row = pl.pallas_call(
        functools.partial(first_kernel, terms),
        out_shape=shaped(
            (blocks, BF16), (blocks, BF16), ((cases, order), F32), ((1, LANES), F32)
        ),
        in_specs=[HBM, VMEM],
        out_specs=[VMEM] * 4,
        scratch_shapes=[
            pltpu.VMEM((order, order), F32),
            pltpu.VMEM((cases, order), F32),
            pltpu.VMEM((ROWS, LANES), F32),
            pltpu.SemaphoreType.DMA((order // CHUNK,)),
        ],
        compiler_params=params(16),
        cost_estimate=pl.CostEstimate(
            flops=4 * cases * order * order, bytes_accessed=8 * order * order, transcendentals=0
        ),
        name="first",
    )(in_hbm(schur[0]), msg)

    half = ((cases, width), F32)
    full = ((cases, order), F32)
    payload = ((devices, slot, LANES), F32)
    rows = ((rows_of(terms * (terms + 1) // 2), LANES), F32)
    near, far, pay_out, mult, masks, pieces = pl.pallas_call(
        functools.partial(second_kernel, terms),
        out_shape=shaped(half, half, payload, full, ((2, order), F32), ((3 * ROWS, order), BF16)),
        in_specs=[VMEM] * 7,
        out_specs=[VMEM] * 6,
        compiler_params=params(8),
        name="second",
    )(high, low, own, halo, msg, load[0], gram_row)

    update = factor = None
    amp_scratch = [pltpu.VMEM((ROWS, LANES), F32)]
    for step in range(ITERS):
        far_in = lax.ppermute(far, AXES, far_pairs)
        near_in = lax.ppermute(near, AXES, near_pairs)
        gathered = lax.all_to_all(pay_out, AXES, 0, 0)
        first = step == 0
        if step < ITERS - 1:
            inputs = [gathered, near, far, near_in, far_in, mult, masks, pieces, load[0], high, low]
            outputs = [half, half, payload, full, full]
            if first:
                outputs.append(rows)
            else:
                inputs += [update, factor]
            out = pl.pallas_call(
                functools.partial(middle_kernel, terms, first, rhos[step]),
                out_shape=shaped(*outputs),
                in_specs=[VMEM] * len(inputs),
                out_specs=[VMEM] * len(outputs),
                scratch_shapes=amp_scratch,
                compiler_params=params(12),
            )(*inputs)
            near, far, pay_out, mult, update = out[:5]
            if first:
                factor = out[5]
        else:
            inputs = [gathered, near, far, near_in, far_in, mult, masks, pieces, update, factor]
            mult, residual, amplitudes = pl.pallas_call(
                functools.partial(last_kernel, terms, rhos[step]),
                out_shape=shaped(half, half, ((terms, cases), F32)),
                in_specs=[VMEM] * len(inputs),
                out_specs=[VMEM] * 3,
                scratch_shapes=amp_scratch,
                compiler_params=params(8),
                name="last",
            )(*inputs)
    return mult[None], residual[None], amplitudes.T


def solution(mesh):
    placed = (
        P(AXES, None, None),
        P(AXES, None, None),
        P(AXES, None, None),
        P(AXES, None, None),
        P(AXES),
        P(AXES),
    )
    return jax.shard_map(
        shards,
        mesh=mesh,
        in_specs=placed,
        out_specs=(P(AXES, None, None), P(AXES, None, None), P()),
        check_vma=False,
    )
```

```python
import functools
import math

import jax
import jax.numpy as jnp
from jax import lax
from jax.experimental import pallas as pl
from jax.experimental.pallas import tpu as pltpu
from jax.sharding import PartitionSpec as P

BLK = 128
ITERS = 3
LOWER = 0.1
UPPER = 8.0
THETA = (LOWER + UPPER) / 2.0
DELTA = (UPPER - LOWER) / 2.0
SIGMA = THETA / DELTA

AXES = ("group", "dev")
LANES = 128
ROWS = 8
CHUNK = 128
DEPTH = 256
WIDE = 256
LAG = 2
F32 = jnp.float32
BF16 = jnp.bfloat16
HIGHEST = lax.Precision.HIGHEST
VMEM = pl.BlockSpec(memory_space=pltpu.VMEM)
SMEM = pl.BlockSpec(memory_space=pltpu.SMEM)
HBM = pl.BlockSpec(memory_space=pltpu.HBM)


def split(x):
    high = x.astype(BF16)
    return high, (x - high.astype(F32)).astype(BF16)


def split3(x):
    high = x.astype(BF16)
    rest = x - high.astype(F32)
    middle = rest.astype(BF16)
    return high, middle, (rest - middle.astype(F32)).astype(BF16)


def dot(a, b):
    return jnp.dot(a, b, preferred_element_type=F32)


def product(x, high, low):
    cases = x.shape[0]
    x_high, x_low = split(x)
    both = dot(jnp.concatenate([x_high, x_low], axis=0), high)
    return both[:cases] + (both[cases:] + dot(x_high, low))


def block_product(both, high_ref, low_ref, start, n):
    cases, depth = both.shape[0] // 2, both.shape[1]
    at = n * (WIDE // LANES)
    high, low = (
        jnp.concatenate([ref[at + p, start : start + depth, :] for p in range(WIDE // LANES)], axis=1)
        for ref in (high_ref, low_ref)
    )
    first = dot(both, high)
    return first[:cases] + (first[cases:] + dot(both[:cases], low))


def position():
    me = lax.axis_index("group") * lax.axis_size("dev") + lax.axis_index("dev")
    return me, lax.axis_size("group") * lax.axis_size("dev")


def pack_kernel(count_ref, from_ref, warm_hbm, modes_hbm, out_ref, warm_ref, modes_ref, sems):
    copies = [
        pltpu.make_async_copy(source, target, sems.at[n])
        for n, (source, target) in enumerate(((warm_hbm, warm_ref), (modes_hbm, modes_ref)))
    ]
    for copy in copies:
        copy.start()
    cases, width = warm_ref.shape
    terms = modes_ref.shape[0]
    spare = out_ref.shape[0] - cases - terms
    dofs = lax.broadcasted_iota(jnp.int32, (1, width), 1)
    alive = dofs < count_ref[0] * BLK
    live = alive.astype(F32)
    contact = (alive & (dofs >= from_ref[0])).astype(F32)
    for copy in copies:
        copy.wait()
    out_ref[:cases, :] = warm_ref[...] * live
    for c in range(terms):
        out_ref[cases + c : cases + c + 1, :] = modes_ref[c] * live
    if spare > 2:
        out_ref[cases + terms :, :] = jnp.zeros((spare, width), F32)
    out_ref[-2:-1, :] = live
    out_ref[-1:, :] = contact


def first_kernel(terms, schur_ref, msg_ref, high_ref, low_ref, own_ref, gram_ref, raw, acc, wide, sems):
    order = schur_ref.shape[0]
    cases = own_ref.shape[0]
    chunks = order // CHUNK
    half = chunks // 2
    sequence = list(range(half, chunks)) + list(range(half))

    def copy(c):
        rows = pl.ds(c * CHUNK, CHUNK)
        return pltpu.make_async_copy(schur_ref.at[rows, :], raw.at[rows, :], sems.at[c])

    for c in sequence:
        copy(c).start()
    modes = msg_ref[cases : cases + ROWS, :]
    modes = jnp.where(lax.broadcasted_iota(jnp.int32, modes.shape, 0) < terms, modes, 0.0)
    wide[...] = jnp.zeros_like(wide)
    wide[:, :ROWS] = lax.dot_general(
        modes, modes, (((1,), (1,)), ((), ())), precision=HIGHEST, preferred_element_type=F32
    )
    row = wide[0:1, :]
    for c in range(1, terms):
        row = row + pltpu.roll(wide[c : c + 1, :], ROWS * c, 1)
    gram_ref[...] = row
    for n, c in enumerate(sequence):
        copy(c).wait()
        rows = pl.ds(c * CHUNK, CHUNK)
        high, low = split(raw[rows, :])
        for j in range(order // LANES):
            lanes = slice(j * LANES, (j + 1) * LANES)
            high_ref[j, c * CHUNK : (c + 1) * CHUNK, :] = high[:, lanes]
            low_ref[j, c * CHUNK : (c + 1) * CHUNK, :] = low[:, lanes]
        if n < half:
            part = product(msg_ref[:cases, n * CHUNK : (n + 1) * CHUNK], high, low)
            if n == 0:
                acc[...] = part
            else:
                acc[...] += part
    own_ref[...] = acc[...]


def finish(block, terms, even, load_ref, pieces, gram_row, near_ref, far_ref, pay_ref):
    cases, width = load_ref.shape
    count = 2 * width // WIDE
    across = (((1,), (1,)), ((), ()))
    z = []
    top = low = 0.0
    for n in range(count + LAG):
        if n < count:
            value = block(n)
            if n * WIDE >= width:
                cols = slice(n * WIDE - width, (n + 1) * WIDE - width)
                partner = z[n - count // 2]
                value = load_ref[:, cols] - value
                near_ref[:, cols] = jnp.where(even, value, partner)
                far_ref[:, cols] = jnp.where(even, partner, value)
            z.append(value)
        if n >= LAG:
            part = pieces[:, (n - LAG) * WIDE : (n - LAG + 1) * WIDE]
            z_high, z_low = split(z[n - LAG])
            top = top + lax.dot_general(part, z_high, across, preferred_element_type=F32)
            low = low + lax.dot_general(part, z_low, across, preferred_element_type=F32)
    coef = top[:ROWS] + ((top[ROWS : 2 * ROWS] + low[:ROWS]) + (top[2 * ROWS : 3 * ROWS] + low[ROWS : 2 * ROWS]))
    per_row = LANES // cases
    used = terms // per_row
    lines = jnp.concatenate([coef[p * used : (p + 1) * used, :] for p in range(per_row)], axis=1)
    slots = pay_ref.shape[0]
    pay_ref[:, :used, :] = jnp.broadcast_to(lines[None], (slots, used, LANES))
    pay_ref[:, used : used + 1, :] = jnp.broadcast_to(gram_row[None], (slots, 1, LANES))


def second_kernel(
    terms, high_ref, low_ref, own_ref, halo_ref, msg_ref, load_ref, gram_ref,
    near_ref, far_ref, pay_ref, mult_ref, mask_ref, pieces_ref,
):
    cases, _ = load_ref.shape
    me, _ = position()
    halo = jnp.where(me > 0, halo_ref[...], 0.0)
    left = halo[:cases]
    tail = halo_ref.shape[0] - 2
    mask_ref[0:2, :] = jnp.concatenate([halo[tail:], msg_ref[tail:, :]], axis=1)
    modes = jnp.concatenate([halo[cases : cases + ROWS], msg_ref[cases : cases + ROWS, :]], axis=1)
    modes = jnp.where(lax.broadcasted_iota(jnp.int32, modes.shape, 0) < terms, modes, 0.0)
    pieces = jnp.concatenate(split3(modes), axis=0)
    pieces_ref[...] = pieces
    both = jnp.concatenate(split(left), axis=0)

    def block(n):
        return own_ref[:, n * WIDE : (n + 1) * WIDE] - block_product(both, high_ref, low_ref, 0, n)

    finish(block, terms, me % 2 == 0, load_ref, pieces, gram_ref[...], near_ref, far_ref, pay_ref)
    mult_ref[...] = jnp.concatenate([left, msg_ref[:cases, :]], axis=1)


def factor_rows(row, terms):
    def entry(c, e):
        lane = ROWS * c + e
        return jnp.broadcast_to(row[:, lane : lane + 1], (1, LANES))

    lower = {}
    inverse = []
    for j in range(terms):
        pivot = entry(j, j)
        for k in range(j):
            pivot = pivot - lower[j, k] * lower[j, k]
        root = jnp.sqrt(pivot)
        inverse.append(1.0 / root)
        for i in range(j + 1, terms):
            value = entry(i, j)
            for k in range(j):
                value = value - lower[i, k] * lower[j, k]
            lower[i, j] = value * inverse[j]
    return lower, inverse


def store_factor(lower, inverse, fac_ref):
    terms = len(inverse)
    n = 0
    for j in range(terms):
        fac_ref[n : n + 1, :] = inverse[j]
        n += 1
    for j in range(terms):
        for i in range(j + 1, terms):
            fac_ref[n : n + 1, :] = lower[i, j]
            n += 1


def load_factor(terms, fac_ref):
    inverse = [fac_ref[j : j + 1, :] for j in range(terms)]
    lower = {}
    n = terms
    for j in range(terms):
        for i in range(j + 1, terms):
            lower[i, j] = fac_ref[n : n + 1, :]
            n += 1
    return lower, inverse


def solve(total, lower, inverse, cases, amp_ref):
    terms = len(inverse)
    per_row = LANES // cases
    used = terms // per_row
    known = []
    for c in range(terms):
        row = total[c % used : c % used + 1, :]
        value = row if c < used else pltpu.roll(row, LANES - (c // used) * cases, 1)
        for k in range(c):
            value = value - lower[c, k] * known[k]
        known.append(value * inverse[c])
    for c in reversed(range(terms)):
        value = known[c]
        for k in range(c + 1, terms):
            value = value - lower[k, c] * known[k]
        known[c] = value * inverse[c]
    amp_ref[...] = jnp.zeros_like(amp_ref)
    for c in range(terms):
        amp_ref[c : c + 1, :] = known[c]
    return amp_ref[...]


def chebyshev(residual, update, rhos):
    rho, rho_new = rhos
    if rho is None:
        return residual / THETA
    return rho_new * rho * update + 2.0 * rho_new / DELTA * residual


def amplitudes_of(amp, cases):
    one, two, three = (p.astype(F32) for p in split3(amp))
    return jnp.transpose(jnp.concatenate([one, two, three, one, two, one], axis=0))[:cases].astype(BF16)


def stacked(pieces):
    m = [pieces[p * ROWS : (p + 1) * ROWS] for p in range(3)]
    return jnp.concatenate([m[0], m[0], m[0], m[1], m[1], m[2]], axis=0)


def middle_kernel(
    terms, first, rhos, sum_ref, near_ref, far_ref, near_in, far_in, mult_ref, mask_ref, pieces_ref, load_ref,
    high_ref, low_ref, *rest,
):
    if first:
        near_out, far_out, pay_ref, mult_out, upd_out, fac_out, amp_ref, coarse_ref = rest
    else:
        upd_ref, fac_ref, near_out, far_out, pay_ref, mult_out, upd_out, amp_ref, coarse_ref = rest
    cases, width = load_ref.shape
    me, devices = position()
    even = me % 2 == 0
    total = jnp.sum(sum_ref[...], axis=0)
    if first:
        used = total.shape[0] - 1
        lower, inverse = factor_rows(total[used : used + 1, :], terms)
        store_factor(lower, inverse, fac_out)
    else:
        lower, inverse = load_factor(terms, fac_ref)
    amp = amplitudes_of(solve(total, lower, inverse, cases, amp_ref), cases)
    pieces = pieces_ref[...]
    coarse_ref[...] = dot(amp, stacked(pieces))
    is_last = me == devices - 1
    y = []
    for start in range(0, 2 * width, DEPTH):
        lanes = slice(start, start + DEPTH)
        half = slice(start % width, start % width + DEPTH)
        near = near_ref[:, half] + near_in[:, half]
        far = far_ref[:, half] + jnp.where(is_last, 0.0, far_in[:, half])
        open_part = jnp.where(even, far, near) if start < width else jnp.where(even, near, far)
        open_part = jnp.where(mask_ref[0:1, lanes] > 0.0, open_part, 0.0)
        residual = open_part - coarse_ref[:, lanes]
        update = chebyshev(residual, None if first else upd_ref[:, lanes], rhos)
        mult = mult_ref[:, lanes] + update
        mult = jnp.where(mask_ref[1:2, lanes] > 0.0, jnp.maximum(mult, 0.0), mult)
        mult_out[:, lanes] = mult
        upd_out[:, lanes] = update
        both = jnp.concatenate(split(-mult if start < width else mult), axis=0)
        if start + DEPTH < 2 * width:
            parts = [block_product(both, high_ref, low_ref, start, n) for n in range(2 * width // WIDE)]
            y = [a + b for a, b in zip(y, parts)] if y else parts

    def block(n):
        return y[n] + block_product(both, high_ref, low_ref, start, n)

    no_gram = jnp.zeros((1, LANES), F32)
    finish(block, terms, even, load_ref, pieces, no_gram, near_out, far_out, pay_ref)


def last_kernel(
    terms, rhos, sum_ref, near_ref, far_ref, near_in, far_in, mult_ref, mask_ref, pieces_ref, upd_ref, fac_ref,
    mult_hbm, res_hbm, amp_out, amp_ref, mult_out, res_out, sems,
):
    cases, width = mult_out.shape
    me, devices = position()
    even = me % 2 == 0
    total = jnp.sum(sum_ref[...], axis=0)
    lower, inverse = load_factor(terms, fac_ref)
    amp = amplitudes_of(solve(total, lower, inverse, cases, amp_ref), cases)
    near = near_ref[...] + near_in[...]
    far = far_ref[...] + jnp.where((me == devices - 1), 0.0, far_in[...])
    live = mask_ref[0:1, width:]
    contact = mask_ref[1:2, width:] > 0.0
    open_part = jnp.where(live > 0.0, jnp.where(even, near, far), 0.0)
    residual = open_part - dot(amp, stacked(pieces_ref[:, width:]))
    res_out[...] = residual
    res_copy = pltpu.make_async_copy(res_out, res_hbm, sems.at[0])
    res_copy.start()
    update = chebyshev(residual, upd_ref[:, width:], rhos)
    mult = mult_ref[:, width:] + update
    mult_out[...] = jnp.where(contact, jnp.maximum(mult, 0.0), mult)
    mult_copy = pltpu.make_async_copy(mult_out, mult_hbm, sems.at[1])
    mult_copy.start()
    amp_out[...] = amp_ref[:terms, :cases]
    res_copy.wait()
    mult_copy.wait()


def rows_of(count):
    return math.ceil(count / ROWS) * ROWS


def shaped(*shapes):
    return [jax.ShapeDtypeStruct(s, d) for s, d in shapes]


def in_hbm(x):
    return pltpu.with_memory_space_constraint(x, pltpu.HBM)


def params(megabytes):
    return pltpu.CompilerParams(vmem_limit_bytes=megabytes << 20)


def shards(schur, coarse_modes, load, warm_start, active_blocks, contact_from):
    _, cases, width = load.shape
    order = schur.shape[1]
    terms = coarse_modes.shape[1]
    devices = lax.axis_size("group") * lax.axis_size("dev")
    blocks = (order // LANES, order, LANES)
    slot = terms // (LANES // cases) + 1
    ring = [(i, (i + 1) % devices) for i in range(devices)]
    near_pairs = [(i, i ^ 1) for i in range(devices)]
    far_pairs = [(i, (i + (1 if i % 2 else devices - 1)) % devices) for i in range(devices)]

    rhos = [(None, None)]
    rho = 1.0 / SIGMA
    for _ in range(1, ITERS):
        rho_new = 1.0 / (2.0 * SIGMA - rho)
        rhos.append((rho, rho_new))
        rho = rho_new

    msg = pl.pallas_call(
        pack_kernel,
        out_shape=jax.ShapeDtypeStruct((rows_of(cases + terms + 2), width), F32),
        in_specs=[SMEM, SMEM, HBM, HBM],
        out_specs=VMEM,
        scratch_shapes=[
            pltpu.VMEM((cases, width), F32),
            pltpu.VMEM((terms, 1, width), F32),
            pltpu.SemaphoreType.DMA((2,)),
        ],
        compiler_params=params(4),
        name="pack",
    )(active_blocks, contact_from, in_hbm(warm_start[0]), in_hbm(jnp.transpose(coarse_modes, (1, 0, 2))))
    halo = lax.ppermute(msg, AXES, ring)
    high, low, own, gram_row = pl.pallas_call(
        functools.partial(first_kernel, terms),
        out_shape=shaped(
            (blocks, BF16), (blocks, BF16), ((cases, order), F32), ((1, LANES), F32)
        ),
        in_specs=[HBM, VMEM],
        out_specs=[VMEM] * 4,
        scratch_shapes=[
            pltpu.VMEM((order, order), F32),
            pltpu.VMEM((cases, order), F32),
            pltpu.VMEM((ROWS, LANES), F32),
            pltpu.SemaphoreType.DMA((order // CHUNK,)),
        ],
        compiler_params=params(16),
        cost_estimate=pl.CostEstimate(
            flops=4 * cases * order * order, bytes_accessed=8 * order * order, transcendentals=0
        ),
        name="first",
    )(in_hbm(schur[0]), msg)

    half = ((cases, width), F32)
    full = ((cases, order), F32)
    payload = ((devices, slot, LANES), F32)
    rows = ((rows_of(terms * (terms + 1) // 2), LANES), F32)
    near, far, pay_out, mult, masks, pieces = pl.pallas_call(
        functools.partial(second_kernel, terms),
        out_shape=shaped(half, half, payload, full, ((2, order), F32), ((3 * ROWS, order), BF16)),
        in_specs=[VMEM] * 7,
        out_specs=[VMEM] * 6,
        compiler_params=params(8),
        name="second",
    )(high, low, own, halo, msg, load[0], gram_row)

    update = factor = None
    amp_scratch = [pltpu.VMEM((ROWS, LANES), F32)]
    for step in range(ITERS):
        far_in = lax.ppermute(far, AXES, far_pairs)
        near_in = lax.ppermute(near, AXES, near_pairs)
        gathered = lax.all_to_all(pay_out, AXES, 0, 0)
        first = step == 0
        if step < ITERS - 1:
            inputs = [gathered, near, far, near_in, far_in, mult, masks, pieces, load[0], high, low]
            outputs = [half, half, payload, full, full]
            if first:
                outputs.append(rows)
            else:
                inputs += [update, factor]
            out = pl.pallas_call(
                functools.partial(middle_kernel, terms, first, rhos[step]),
                out_shape=shaped(*outputs),
                in_specs=[VMEM] * len(inputs),
                out_specs=[VMEM] * len(outputs),
                scratch_shapes=amp_scratch + [pltpu.VMEM((cases, order), F32)],
                compiler_params=params(12),
            )(*inputs)
            near, far, pay_out, mult, update = out[:5]
            if first:
                factor = out[5]
        else:
            inputs = [gathered, near, far, near_in, far_in, mult, masks, pieces, update, factor]
            mult, residual, amplitudes = pl.pallas_call(
                functools.partial(last_kernel, terms, rhos[step]),
                out_shape=shaped(half, half, ((terms, cases), F32)),
                in_specs=[VMEM] * len(inputs),
                out_specs=[HBM, HBM, VMEM],
                scratch_shapes=amp_scratch
                + [pltpu.VMEM((cases, width), F32)] * 2
                + [pltpu.SemaphoreType.DMA((2,))],
                compiler_params=params(8),
                name="last",
            )(*inputs)
    return mult[None], residual[None], amplitudes.T


def solution(mesh):
    placed = (
        P(AXES, None, None),
        P(AXES, None, None),
        P(AXES, None, None),
        P(AXES, None, None),
        P(AXES),
        P(AXES),
    )
    return jax.shard_map(
        shards,
        mesh=mesh,
        in_specs=placed,
        out_specs=(P(AXES, None, None), P(AXES, None, None), P()),
        check_vma=False,
    )
```

```python
import functools
import math

import jax
import jax.numpy as jnp
from jax import lax
from jax.experimental import pallas as pl
from jax.experimental.pallas import tpu as pltpu
from jax.sharding import PartitionSpec as P

BLK = 128
ITERS = 3
LOWER = 0.1
UPPER = 8.0
THETA = (LOWER + UPPER) / 2.0
DELTA = (UPPER - LOWER) / 2.0
SIGMA = THETA / DELTA

AXES = ("group", "dev")
LANES = 128
ROWS = 8
CHUNK = 128
DEPTH = 256
WIDE = 256
LAG = 2
F32 = jnp.float32
BF16 = jnp.bfloat16
HIGHEST = lax.Precision.HIGHEST
VMEM = pl.BlockSpec(memory_space=pltpu.VMEM)
SMEM = pl.BlockSpec(memory_space=pltpu.SMEM)
HBM = pl.BlockSpec(memory_space=pltpu.HBM)


def split(x):
    high = x.astype(BF16)
    return high, (x - high.astype(F32)).astype(BF16)


def split3(x):
    high = x.astype(BF16)
    rest = x - high.astype(F32)
    middle = rest.astype(BF16)
    return high, middle, (rest - middle.astype(F32)).astype(BF16)


def dot(a, b):
    return jnp.dot(a, b, preferred_element_type=F32)


def product(x, high, low):
    cases = x.shape[0]
    x_high, x_low = split(x)
    both = dot(jnp.concatenate([x_high, x_low], axis=0), high)
    return both[:cases] + (both[cases:] + dot(x_high, low))


def block_product(both, high_ref, low_ref, start, n):
    cases, depth = both.shape[0] // 2, both.shape[1]
    at = n * (WIDE // LANES)
    high, low = (
        jnp.concatenate([ref[at + p, start : start + depth, :] for p in range(WIDE // LANES)], axis=1)
        for ref in (high_ref, low_ref)
    )
    first = dot(both, high)
    return first[:cases] + (first[cases:] + dot(both[:cases], low))


def position():
    me = lax.axis_index("group") * lax.axis_size("dev") + lax.axis_index("dev")
    return me, lax.axis_size("group") * lax.axis_size("dev")


def pack_kernel(count_ref, from_ref, warm_hbm, modes_hbm, out_ref, warm_ref, modes_ref, sems):
    copies = [
        pltpu.make_async_copy(source, target, sems.at[n])
        for n, (source, target) in enumerate(((warm_hbm, warm_ref), (modes_hbm, modes_ref)))
    ]
    for copy in copies:
        copy.start()
    cases, width = warm_ref.shape
    terms = modes_ref.shape[0]
    spare = out_ref.shape[0] - cases - terms
    dofs = lax.broadcasted_iota(jnp.int32, (1, width), 1)
    alive = dofs < count_ref[0] * BLK
    live = alive.astype(F32)
    contact = (alive & (dofs >= from_ref[0])).astype(F32)
    for copy in copies:
        copy.wait()
    out_ref[:cases, :] = warm_ref[...] * live
    for c in range(terms):
        out_ref[cases + c : cases + c + 1, :] = modes_ref[c] * live
    if spare > 2:
        out_ref[cases + terms :, :] = jnp.zeros((spare, width), F32)
    out_ref[-2:-1, :] = live
    out_ref[-1:, :] = contact


def first_kernel(terms, schur_ref, msg_ref, high_ref, low_ref, own_ref, gram_ref, raw, acc, wide, sems):
    order = schur_ref.shape[0]
    cases = own_ref.shape[0]
    chunks = order // CHUNK
    half = chunks // 2
    sequence = list(range(half, chunks)) + list(range(half))

    def copy(c):
        rows = pl.ds(c * CHUNK, CHUNK)
        return pltpu.make_async_copy(schur_ref.at[rows, :], raw.at[rows, :], sems.at[c])

    for c in sequence:
        copy(c).start()
    modes = msg_ref[cases : cases + ROWS, :]
    modes = jnp.where(lax.broadcasted_iota(jnp.int32, modes.shape, 0) < terms, modes, 0.0)
    wide[...] = jnp.zeros_like(wide)
    wide[:, :ROWS] = lax.dot_general(
        modes, modes, (((1,), (1,)), ((), ())), precision=HIGHEST, preferred_element_type=F32
    )
    row = wide[0:1, :]
    for c in range(1, terms):
        row = row + pltpu.roll(wide[c : c + 1, :], ROWS * c, 1)
    gram_ref[...] = row
    for n, c in enumerate(sequence):
        copy(c).wait()
        rows = pl.ds(c * CHUNK, CHUNK)
        high, low = split(raw[rows, :])
        for j in range(order // LANES):
            lanes = slice(j * LANES, (j + 1) * LANES)
            high_ref[j, c * CHUNK : (c + 1) * CHUNK, :] = high[:, lanes]
            low_ref[j, c * CHUNK : (c + 1) * CHUNK, :] = low[:, lanes]
        if n < half:
            part = product(msg_ref[:cases, n * CHUNK : (n + 1) * CHUNK], high, low)
            if n == 0:
                acc[...] = part
            else:
                acc[...] += part
    own_ref[...] = acc[...]


def finish(block, terms, even, load_ref, pieces, gram_row, near_ref, far_ref, pay_ref):
    cases, width = load_ref.shape
    count = 2 * width // WIDE
    across = (((1,), (1,)), ((), ()))
    z = []
    top = low = 0.0
    for n in range(count + LAG):
        if n < count:
            value = block(n)
            if n * WIDE >= width:
                cols = slice(n * WIDE - width, (n + 1) * WIDE - width)
                partner = z[n - count // 2]
                value = load_ref[:, cols] - value
                near_ref[:, cols] = value if even is None else jnp.where(even, value, partner)
                far_ref[:, cols] = partner if even is None else jnp.where(even, partner, value)
            z.append(value)
        if n >= LAG:
            part = pieces[:, (n - LAG) * WIDE : (n - LAG + 1) * WIDE]
            z_high, z_low = split(z[n - LAG])
            top = top + lax.dot_general(part, z_high, across, preferred_element_type=F32)
            low = low + lax.dot_general(part, z_low, across, preferred_element_type=F32)
    coef = top[:ROWS] + ((top[ROWS : 2 * ROWS] + low[:ROWS]) + (top[2 * ROWS : 3 * ROWS] + low[ROWS : 2 * ROWS]))
    per_row = LANES // cases
    used = terms // per_row
    lines = jnp.concatenate([coef[p * used : (p + 1) * used, :] for p in range(per_row)], axis=1)
    slots = pay_ref.shape[0]
    pay_ref[:, :used, :] = jnp.broadcast_to(lines[None], (slots, used, LANES))
    pay_ref[:, used : used + 1, :] = jnp.broadcast_to(gram_row[None], (slots, 1, LANES))


def second_kernel(
    terms, high_ref, low_ref, own_ref, halo_ref, msg_ref, load_ref, gram_ref,
    near_ref, far_ref, pay_ref, mult_ref, mask_ref, pieces_ref,
):
    cases, _ = load_ref.shape
    me, _ = position()
    halo = jnp.where(me > 0, halo_ref[...], 0.0)
    left = halo[:cases]
    tail = halo_ref.shape[0] - 2
    mask_ref[0:2, :] = jnp.concatenate([halo[tail:], msg_ref[tail:, :]], axis=1)
    modes = jnp.concatenate([halo[cases : cases + ROWS], msg_ref[cases : cases + ROWS, :]], axis=1)
    modes = jnp.where(lax.broadcasted_iota(jnp.int32, modes.shape, 0) < terms, modes, 0.0)
    pieces = jnp.concatenate(split3(modes), axis=0)
    pieces_ref[...] = pieces
    both = jnp.concatenate(split(left), axis=0)

    def block(n):
        return own_ref[:, n * WIDE : (n + 1) * WIDE] - block_product(both, high_ref, low_ref, 0, n)

    finish(block, terms, me % 2 == 0, load_ref, pieces, gram_ref[...], near_ref, far_ref, pay_ref)
    mult_ref[...] = jnp.concatenate([left, msg_ref[:cases, :]], axis=1)


def factor_rows(row, terms):
    def entry(c, e):
        lane = ROWS * c + e
        return jnp.broadcast_to(row[:, lane : lane + 1], (1, LANES))

    lower = {}
    inverse = []
    for j in range(terms):
        pivot = entry(j, j)
        for k in range(j):
            pivot = pivot - lower[j, k] * lower[j, k]
        root = jnp.sqrt(pivot)
        inverse.append(1.0 / root)
        for i in range(j + 1, terms):
            value = entry(i, j)
            for k in range(j):
                value = value - lower[i, k] * lower[j, k]
            lower[i, j] = value * inverse[j]
    return lower, inverse


def store_factor(lower, inverse, fac_ref):
    terms = len(inverse)
    n = 0
    for j in range(terms):
        fac_ref[n : n + 1, :] = inverse[j]
        n += 1
    for j in range(terms):
        for i in range(j + 1, terms):
            fac_ref[n : n + 1, :] = lower[i, j]
            n += 1


def load_factor(terms, fac_ref):
    inverse = [fac_ref[j : j + 1, :] for j in range(terms)]
    lower = {}
    n = terms
    for j in range(terms):
        for i in range(j + 1, terms):
            lower[i, j] = fac_ref[n : n + 1, :]
            n += 1
    return lower, inverse


def solve(total, lower, inverse, cases, amp_ref):
    terms = len(inverse)
    per_row = LANES // cases
    used = terms // per_row
    known = []
    for c in range(terms):
        row = total[c % used : c % used + 1, :]
        value = row if c < used else pltpu.roll(row, LANES - (c // used) * cases, 1)
        for k in range(c):
            value = value - lower[c, k] * known[k]
        known.append(value * inverse[c])
    for c in reversed(range(terms)):
        value = known[c]
        for k in range(c + 1, terms):
            value = value - lower[k, c] * known[k]
        known[c] = value * inverse[c]
    amp_ref[...] = jnp.zeros_like(amp_ref)
    for c in range(terms):
        amp_ref[c : c + 1, :] = known[c]
    return amp_ref[...]


def chebyshev(residual, update, rhos):
    rho, rho_new = rhos
    if rho is None:
        return residual / THETA
    return rho_new * rho * update + 2.0 * rho_new / DELTA * residual


def amplitudes_of(amp, cases):
    one, two, three = (p.astype(F32) for p in split3(amp))
    return jnp.transpose(jnp.concatenate([one, two, three, one, two, one], axis=0))[:cases].astype(BF16)


def stacked(pieces):
    m = [pieces[p * ROWS : (p + 1) * ROWS] for p in range(3)]
    return jnp.concatenate([m[0], m[0], m[0], m[1], m[1], m[2]], axis=0)


def middle_kernel(
    terms, first, pairs, rhos, sum_ref, near_ref, far_ref, near_in, far_in, mult_ref, mask_ref, pieces_ref, load_ref,
    high_ref, low_ref, *rest,
):
    if first:
        near_out, far_out, pay_ref, mult_out, upd_out, fac_out, amp_ref, coarse_ref = rest
    else:
        upd_ref, fac_ref, near_out, far_out, pay_ref, mult_out, upd_out, amp_ref, coarse_ref = rest
    cases, width = load_ref.shape
    me, devices = position()
    even = me % 2 == 0
    total = jnp.sum(sum_ref[...], axis=0)
    if first:
        used = total.shape[0] - 1
        lower, inverse = factor_rows(total[used : used + 1, :], terms)
        store_factor(lower, inverse, fac_out)
    else:
        lower, inverse = load_factor(terms, fac_ref)
    amp = amplitudes_of(solve(total, lower, inverse, cases, amp_ref), cases)
    pieces = pieces_ref[...]
    coarse_ref[...] = dot(amp, stacked(pieces))
    is_last = me == devices - 1
    y = []
    for start in range(0, 2 * width, DEPTH):
        lanes = slice(start, start + DEPTH)
        half = slice(start % width, start % width + DEPTH)
        near = near_ref[:, half] + near_in[:, half]
        far = far_ref[:, half] + jnp.where(is_last, 0.0, far_in[:, half])
        open_part = jnp.where(even, far, near) if start < width else jnp.where(even, near, far)
        open_part = jnp.where(mask_ref[0:1, lanes] > 0.0, open_part, 0.0)
        residual = open_part - coarse_ref[:, lanes]
        update = chebyshev(residual, None if first else upd_ref[:, lanes], rhos)
        mult = mult_ref[:, lanes] + update
        mult = jnp.where(mask_ref[1:2, lanes] > 0.0, jnp.maximum(mult, 0.0), mult)
        mult_out[:, lanes] = mult
        upd_out[:, lanes] = update
        both = jnp.concatenate(split(-mult if start < width else mult), axis=0)
        if start + DEPTH < 2 * width:
            parts = [block_product(both, high_ref, low_ref, start, n) for n in range(2 * width // WIDE)]
            y = [a + b for a, b in zip(y, parts)] if y else parts

    def block(n):
        return y[n] + block_product(both, high_ref, low_ref, start, n)

    no_gram = jnp.zeros((1, LANES), F32)
    finish(block, terms, even if pairs else None, load_ref, pieces, no_gram, near_out, far_out, pay_ref)


def last_kernel(
    terms, rhos, sum_ref, own_ref, next_in, mult_ref, mask_ref, pieces_ref, upd_ref, fac_ref,
    mult_out, res_out, amp_out, amp_ref,
):
    cases, width = mult_out.shape
    me, devices = position()
    total = jnp.sum(sum_ref[...], axis=0)
    lower, inverse = load_factor(terms, fac_ref)
    amp = amplitudes_of(solve(total, lower, inverse, cases, amp_ref), cases)
    open_part = own_ref[...] + jnp.where(me == devices - 1, 0.0, next_in[...])
    live = mask_ref[0:1, width:]
    contact = mask_ref[1:2, width:] > 0.0
    open_part = jnp.where(live > 0.0, open_part, 0.0)
    residual = open_part - dot(amp, stacked(pieces_ref[:, width:]))
    res_out[...] = residual
    update = chebyshev(residual, upd_ref[:, width:], rhos)
    mult = mult_ref[:, width:] + update
    mult_out[...] = jnp.where(contact, jnp.maximum(mult, 0.0), mult)
    amp_out[...] = amp_ref[:terms, :cases]


def rows_of(count):
    return math.ceil(count / ROWS) * ROWS


def shaped(*shapes):
    return [jax.ShapeDtypeStruct(s, d) for s, d in shapes]


def in_hbm(x):
    return pltpu.with_memory_space_constraint(x, pltpu.HBM)


def params(megabytes):
    return pltpu.CompilerParams(vmem_limit_bytes=megabytes << 20)


def shards(schur, coarse_modes, load, warm_start, active_blocks, contact_from):
    _, cases, width = load.shape
    order = schur.shape[1]
    terms = coarse_modes.shape[1]
    devices = lax.axis_size("group") * lax.axis_size("dev")
    blocks = (order // LANES, order, LANES)
    slot = terms // (LANES // cases) + 1
    ring = [(i, (i + 1) % devices) for i in range(devices)]
    back = [(target, source) for source, target in ring]
    near_pairs = [(i, i ^ 1) for i in range(devices)]
    far_pairs = [(i, (i + (1 if i % 2 else devices - 1)) % devices) for i in range(devices)]

    rhos = [(None, None)]
    rho = 1.0 / SIGMA
    for _ in range(1, ITERS):
        rho_new = 1.0 / (2.0 * SIGMA - rho)
        rhos.append((rho, rho_new))
        rho = rho_new

    msg = pl.pallas_call(
        pack_kernel,
        out_shape=jax.ShapeDtypeStruct((rows_of(cases + terms + 2), width), F32),
        in_specs=[SMEM, SMEM, HBM, HBM],
        out_specs=VMEM,
        scratch_shapes=[
            pltpu.VMEM((cases, width), F32),
            pltpu.VMEM((terms, 1, width), F32),
            pltpu.SemaphoreType.DMA((2,)),
        ],
        compiler_params=params(4),
        name="pack",
    )(active_blocks, contact_from, in_hbm(warm_start[0]), in_hbm(jnp.transpose(coarse_modes, (1, 0, 2))))
    halo = lax.ppermute(msg, AXES, ring)
    high, low, own, gram_row = pl.pallas_call(
        functools.partial(first_kernel, terms),
        out_shape=shaped(
            (blocks, BF16), (blocks, BF16), ((cases, order), F32), ((1, LANES), F32)
        ),
        in_specs=[HBM, VMEM],
        out_specs=[VMEM] * 4,
        scratch_shapes=[
            pltpu.VMEM((order, order), F32),
            pltpu.VMEM((cases, order), F32),
            pltpu.VMEM((ROWS, LANES), F32),
            pltpu.SemaphoreType.DMA((order // CHUNK,)),
        ],
        compiler_params=params(16),
        cost_estimate=pl.CostEstimate(
            flops=4 * cases * order * order, bytes_accessed=8 * order * order, transcendentals=0
        ),
        name="first",
    )(in_hbm(schur[0]), msg)

    half = ((cases, width), F32)
    full = ((cases, order), F32)
    payload = ((devices, slot, LANES), F32)
    rows = ((rows_of(terms * (terms + 1) // 2), LANES), F32)
    near, far, pay_out, mult, masks, pieces = pl.pallas_call(
        functools.partial(second_kernel, terms),
        out_shape=shaped(half, half, payload, full, ((2, order), F32), ((3 * ROWS, order), BF16)),
        in_specs=[VMEM] * 7,
        out_specs=[VMEM] * 6,
        compiler_params=params(8),
        name="second",
    )(high, low, own, halo, msg, load[0], gram_row)

    update = factor = None
    amp_scratch = [pltpu.VMEM((ROWS, LANES), F32)]
    for step in range(ITERS):
        far_in = lax.ppermute(far, AXES, far_pairs if step < ITERS - 1 else back)
        if step < ITERS - 1:
            near_in = lax.ppermute(near, AXES, near_pairs)
        gathered = lax.all_to_all(pay_out, AXES, 0, 0)
        first = step == 0
        if step < ITERS - 1:
            inputs = [gathered, near, far, near_in, far_in, mult, masks, pieces, load[0], high, low]
            outputs = [half, half, payload, full, full]
            if first:
                outputs.append(rows)
            else:
                inputs += [update, factor]
            out = pl.pallas_call(
                functools.partial(middle_kernel, terms, first, step < ITERS - 2, rhos[step]),
                out_shape=shaped(*outputs),
                in_specs=[VMEM] * len(inputs),
                out_specs=[VMEM] * len(outputs),
                scratch_shapes=amp_scratch + [pltpu.VMEM((cases, order), F32)],
                compiler_params=params(12),
            )(*inputs)
            near, far, pay_out, mult, update = out[:5]
            if first:
                factor = out[5]
        else:
            inputs = [gathered, near, far_in, mult, masks, pieces, update, factor]
            mult, residual, amplitudes = pl.pallas_call(
                functools.partial(last_kernel, terms, rhos[step]),
                out_shape=shaped(half, half, ((terms, cases), F32)),
                in_specs=[VMEM] * len(inputs),
                out_specs=[VMEM] * 3,
                scratch_shapes=amp_scratch,
                compiler_params=params(8),
                name="last",
            )(*inputs)
    return mult[None], residual[None], amplitudes.T


def solution(mesh):
    placed = (
        P(AXES, None, None),
        P(AXES, None, None),
        P(AXES, None, None),
        P(AXES, None, None),
        P(AXES),
        P(AXES),
    )
    return jax.shard_map(
        shards,
        mesh=mesh,
        in_specs=placed,
        out_specs=(P(AXES, None, None), P(AXES, None, None), P()),
        check_vma=False,
    )
```

```python
import functools
import math

import jax
import jax.numpy as jnp
from jax import lax
from jax.experimental import pallas as pl
from jax.experimental.pallas import tpu as pltpu
from jax.sharding import PartitionSpec as P

BLK = 128
ITERS = 3
LOWER = 0.1
UPPER = 8.0
THETA = (LOWER + UPPER) / 2.0
DELTA = (UPPER - LOWER) / 2.0
SIGMA = THETA / DELTA

AXES = ("group", "dev")
LANES = 128
ROWS = 8
CHUNK = 128
DEPTH = 256
WIDE = 256
LAG = 2
F32 = jnp.float32
BF16 = jnp.bfloat16
HIGHEST = lax.Precision.HIGHEST
VMEM = pl.BlockSpec(memory_space=pltpu.VMEM)
SMEM = pl.BlockSpec(memory_space=pltpu.SMEM)
HBM = pl.BlockSpec(memory_space=pltpu.HBM)


def split(x):
    high = x.astype(BF16)
    return high, (x - high.astype(F32)).astype(BF16)


def split3(x):
    high = x.astype(BF16)
    rest = x - high.astype(F32)
    middle = rest.astype(BF16)
    return high, middle, (rest - middle.astype(F32)).astype(BF16)


def dot(a, b):
    return jnp.dot(a, b, preferred_element_type=F32)


def product(x, high, low):
    cases = x.shape[0]
    x_high, x_low = split(x)
    both = dot(jnp.concatenate([x_high, x_low], axis=0), high)
    return both[:cases] + (both[cases:] + dot(x_high, low))


def block_product(both, high_ref, low_ref, start, n):
    cases, depth = both.shape[0] // 2, both.shape[1]
    at = n * (WIDE // LANES)
    high, low = (
        jnp.concatenate([ref[at + p, start : start + depth, :] for p in range(WIDE // LANES)], axis=1)
        for ref in (high_ref, low_ref)
    )
    first = dot(both, high)
    return first[:cases] + (first[cases:] + dot(both[:cases], low))


def position():
    me = lax.axis_index("group") * lax.axis_size("dev") + lax.axis_index("dev")
    return me, lax.axis_size("group") * lax.axis_size("dev")


def pack_kernel(count_ref, from_ref, warm_hbm, modes_hbm, out_ref, tail_ref, warm_ref, modes_ref, sems):
    copies = [
        pltpu.make_async_copy(source, target, sems.at[n])
        for n, (source, target) in enumerate(((warm_hbm, warm_ref), (modes_hbm, modes_ref)))
    ]
    for copy in copies:
        copy.start()
    _, width = warm_ref.shape
    terms = modes_ref.shape[0]
    spare = tail_ref.shape[0] - terms
    dofs = lax.broadcasted_iota(jnp.int32, (1, width), 1)
    alive = dofs < count_ref[0] * BLK
    live = alive.astype(F32)
    contact = (alive & (dofs >= from_ref[0])).astype(F32)
    for copy in copies:
        copy.wait()
    out_ref[...] = warm_ref[...] * live
    for c in range(terms):
        tail_ref[c : c + 1, :] = modes_ref[c] * live
    if spare > 2:
        tail_ref[terms:, :] = jnp.zeros((spare, width), F32)
    tail_ref[-2:-1, :] = live
    tail_ref[-1:, :] = contact


def first_kernel(terms, schur_ref, msg_ref, tail_ref, high_ref, low_ref, own_ref, gram_ref, raw, acc, wide, sems):
    order = schur_ref.shape[0]
    chunks = order // CHUNK
    half = chunks // 2
    sequence = list(range(half, chunks)) + list(range(half))

    def copy(c):
        rows = pl.ds(c * CHUNK, CHUNK)
        return pltpu.make_async_copy(schur_ref.at[rows, :], raw.at[rows, :], sems.at[c])

    for c in sequence:
        copy(c).start()
    modes = tail_ref[:ROWS, :]
    modes = jnp.where(lax.broadcasted_iota(jnp.int32, modes.shape, 0) < terms, modes, 0.0)
    wide[...] = jnp.zeros_like(wide)
    wide[:, :ROWS] = lax.dot_general(
        modes, modes, (((1,), (1,)), ((), ())), precision=HIGHEST, preferred_element_type=F32
    )
    row = wide[0:1, :]
    for c in range(1, terms):
        row = row + pltpu.roll(wide[c : c + 1, :], ROWS * c, 1)
    gram_ref[...] = row
    for n, c in enumerate(sequence):
        copy(c).wait()
        rows = pl.ds(c * CHUNK, CHUNK)
        high, low = split(raw[rows, :])
        for j in range(order // LANES):
            lanes = slice(j * LANES, (j + 1) * LANES)
            high_ref[j, c * CHUNK : (c + 1) * CHUNK, :] = high[:, lanes]
            low_ref[j, c * CHUNK : (c + 1) * CHUNK, :] = low[:, lanes]
        if n < half:
            part = product(msg_ref[:, n * CHUNK : (n + 1) * CHUNK], high, low)
            if n == 0:
                acc[...] = part
            else:
                acc[...] += part
    own_ref[...] = acc[...]


def finish(block, terms, even, load_ref, pieces, gram_row, near_ref, far_ref, pay_ref):
    cases, width = load_ref.shape
    count = 2 * width // WIDE
    across = (((1,), (1,)), ((), ()))
    z = []
    top = low = 0.0
    for n in range(count + LAG):
        if n < count:
            value = block(n)
            if n * WIDE >= width:
                cols = slice(n * WIDE - width, (n + 1) * WIDE - width)
                partner = z[n - count // 2]
                value = load_ref[:, cols] - value
                near_ref[:, cols] = value if even is None else jnp.where(even, value, partner)
                far_ref[:, cols] = partner if even is None else jnp.where(even, partner, value)
            z.append(value)
        if n >= LAG:
            part = pieces[:, (n - LAG) * WIDE : (n - LAG + 1) * WIDE]
            z_high, z_low = split(z[n - LAG])
            top = top + lax.dot_general(part, z_high, across, preferred_element_type=F32)
            low = low + lax.dot_general(part, z_low, across, preferred_element_type=F32)
    coef = top[:ROWS] + ((top[ROWS : 2 * ROWS] + low[:ROWS]) + (top[2 * ROWS : 3 * ROWS] + low[ROWS : 2 * ROWS]))
    per_row = LANES // cases
    used = terms // per_row
    lines = jnp.concatenate([coef[p * used : (p + 1) * used, :] for p in range(per_row)], axis=1)
    slots = pay_ref.shape[0]
    pay_ref[:, :used, :] = jnp.broadcast_to(lines[None], (slots, used, LANES))
    pay_ref[:, used : used + 1, :] = jnp.broadcast_to(gram_row[None], (slots, 1, LANES))


def second_kernel(
    terms, high_ref, low_ref, own_ref, halo_ref, halo_tail_ref, msg_ref, tail_ref, load_ref, gram_ref,
    near_ref, far_ref, pay_ref, mult_ref, mask_ref, pieces_ref,
):
    me, _ = position()
    halo_tail = jnp.where(me > 0, halo_tail_ref[...], 0.0)
    left = jnp.where(halo_tail[-2:-1] > 0.0, halo_ref[...], 0.0)
    mask_ref[...] = jnp.concatenate([halo_tail[-2:], tail_ref[-2:, :]], axis=1)
    modes = jnp.concatenate([halo_tail[:ROWS], tail_ref[:ROWS, :]], axis=1)
    modes = jnp.where(lax.broadcasted_iota(jnp.int32, modes.shape, 0) < terms, modes, 0.0)
    pieces = jnp.concatenate(split3(modes), axis=0)
    pieces_ref[...] = pieces
    both = jnp.concatenate(split(left), axis=0)

    def block(n):
        return own_ref[:, n * WIDE : (n + 1) * WIDE] - block_product(both, high_ref, low_ref, 0, n)

    finish(block, terms, me % 2 == 0, load_ref, pieces, gram_ref[...], near_ref, far_ref, pay_ref)
    mult_ref[...] = jnp.concatenate([left, msg_ref[...]], axis=1)


def factor_rows(row, terms):
    def entry(c, e):
        lane = ROWS * c + e
        return jnp.broadcast_to(row[:, lane : lane + 1], (1, LANES))

    lower = {}
    inverse = []
    for j in range(terms):
        pivot = entry(j, j)
        for k in range(j):
            pivot = pivot - lower[j, k] * lower[j, k]
        root = jnp.sqrt(pivot)
        inverse.append(1.0 / root)
        for i in range(j + 1, terms):
            value = entry(i, j)
            for k in range(j):
                value = value - lower[i, k] * lower[j, k]
            lower[i, j] = value * inverse[j]
    return lower, inverse


def store_factor(lower, inverse, fac_ref):
    terms = len(inverse)
    n = 0
    for j in range(terms):
        fac_ref[n : n + 1, :] = inverse[j]
        n += 1
    for j in range(terms):
        for i in range(j + 1, terms):
            fac_ref[n : n + 1, :] = lower[i, j]
            n += 1


def load_factor(terms, fac_ref):
    inverse = [fac_ref[j : j + 1, :] for j in range(terms)]
    lower = {}
    n = terms
    for j in range(terms):
        for i in range(j + 1, terms):
            lower[i, j] = fac_ref[n : n + 1, :]
            n += 1
    return lower, inverse


def solve(total, lower, inverse, cases, amp_ref):
    terms = len(inverse)
    per_row = LANES // cases
    used = terms // per_row
    known = []
    for c in range(terms):
        row = total[c % used : c % used + 1, :]
        value = row if c < used else pltpu.roll(row, LANES - (c // used) * cases, 1)
        for k in range(c):
            value = value - lower[c, k] * known[k]
        known.append(value * inverse[c])
    for c in reversed(range(terms)):
        value = known[c]
        for k in range(c + 1, terms):
            value = value - lower[k, c] * known[k]
        known[c] = value * inverse[c]
    amp_ref[...] = jnp.zeros_like(amp_ref)
    for c in range(terms):
        amp_ref[c : c + 1, :] = known[c]
    return amp_ref[...]


def chebyshev(residual, update, rhos):
    rho, rho_new = rhos
    if rho is None:
        return residual / THETA
    return rho_new * rho * update + 2.0 * rho_new / DELTA * residual


def amplitudes_of(amp, cases):
    one, two, three = (p.astype(F32) for p in split3(amp))
    return jnp.transpose(jnp.concatenate([one, two, three, one, two, one], axis=0))[:cases].astype(BF16)


def stacked(pieces):
    m = [pieces[p * ROWS : (p + 1) * ROWS] for p in range(3)]
    return jnp.concatenate([m[0], m[0], m[0], m[1], m[1], m[2]], axis=0)


def middle_kernel(
    terms, first, pairs, rhos, sum_ref, near_ref, far_ref, near_in, far_in, mult_ref, mask_ref, pieces_ref, load_ref,
    high_ref, low_ref, *rest,
):
    if first:
        near_out, far_out, pay_ref, mult_out, upd_out, fac_out, amp_ref, coarse_ref = rest
    else:
        upd_ref, fac_ref, near_out, far_out, pay_ref, mult_out, upd_out, amp_ref, coarse_ref = rest
    cases, width = load_ref.shape
    me, devices = position()
    even = me % 2 == 0
    total = jnp.sum(sum_ref[...], axis=0)
    if first:
        used = total.shape[0] - 1
        lower, inverse = factor_rows(total[used : used + 1, :], terms)
        store_factor(lower, inverse, fac_out)
    else:
        lower, inverse = load_factor(terms, fac_ref)
    amp = amplitudes_of(solve(total, lower, inverse, cases, amp_ref), cases)
    pieces = pieces_ref[...]
    coarse_ref[...] = dot(amp, stacked(pieces))
    is_last = me == devices - 1
    y = []
    for start in range(0, 2 * width, DEPTH):
        lanes = slice(start, start + DEPTH)
        half = slice(start % width, start % width + DEPTH)
        near = near_ref[:, half] + near_in[:, half]
        far = far_ref[:, half] + jnp.where(is_last, 0.0, far_in[:, half])
        open_part = jnp.where(even, far, near) if start < width else jnp.where(even, near, far)
        open_part = jnp.where(mask_ref[0:1, lanes] > 0.0, open_part, 0.0)
        residual = open_part - coarse_ref[:, lanes]
        update = chebyshev(residual, None if first else upd_ref[:, lanes], rhos)
        mult = mult_ref[:, lanes] + update
        mult = jnp.where(mask_ref[1:2, lanes] > 0.0, jnp.maximum(mult, 0.0), mult)
        mult_out[:, lanes] = mult
        upd_out[:, lanes] = update
        both = jnp.concatenate(split(-mult if start < width else mult), axis=0)
        if start + DEPTH < 2 * width:
            parts = [block_product(both, high_ref, low_ref, start, n) for n in range(2 * width // WIDE)]
            y = [a + b for a, b in zip(y, parts)] if y else parts

    def block(n):
        return y[n] + block_product(both, high_ref, low_ref, start, n)

    no_gram = jnp.zeros((1, LANES), F32)
    finish(block, terms, even if pairs else None, load_ref, pieces, no_gram, near_out, far_out, pay_ref)


def last_kernel(
    terms, rhos, sum_ref, own_ref, next_in, mult_ref, mask_ref, pieces_ref, upd_ref, fac_ref,
    mult_out, res_out, amp_out, amp_ref,
):
    cases, width = mult_out.shape
    me, devices = position()
    total = jnp.sum(sum_ref[...], axis=0)
    lower, inverse = load_factor(terms, fac_ref)
    amp = amplitudes_of(solve(total, lower, inverse, cases, amp_ref), cases)
    open_part = own_ref[...] + jnp.where(me == devices - 1, 0.0, next_in[...])
    live = mask_ref[0:1, width:]
    contact = mask_ref[1:2, width:] > 0.0
    open_part = jnp.where(live > 0.0, open_part, 0.0)
    residual = open_part - dot(amp, stacked(pieces_ref[:, width:]))
    res_out[...] = residual
    update = chebyshev(residual, upd_ref[:, width:], rhos)
    mult = mult_ref[:, width:] + update
    mult_out[...] = jnp.where(contact, jnp.maximum(mult, 0.0), mult)
    amp_out[...] = amp_ref[:terms, :cases]


def rows_of(count):
    return math.ceil(count / ROWS) * ROWS


def shaped(*shapes):
    return [jax.ShapeDtypeStruct(s, d) for s, d in shapes]


def in_hbm(x):
    return pltpu.with_memory_space_constraint(x, pltpu.HBM)


def params(megabytes):
    return pltpu.CompilerParams(vmem_limit_bytes=megabytes << 20)


def shards(schur, coarse_modes, load, warm_start, active_blocks, contact_from):
    _, cases, width = load.shape
    order = schur.shape[1]
    terms = coarse_modes.shape[1]
    devices = lax.axis_size("group") * lax.axis_size("dev")
    blocks = (order // LANES, order, LANES)
    slot = terms // (LANES // cases) + 1
    ring = [(i, (i + 1) % devices) for i in range(devices)]
    back = [(target, source) for source, target in ring]
    near_pairs = [(i, i ^ 1) for i in range(devices)]
    far_pairs = [(i, (i + (1 if i % 2 else devices - 1)) % devices) for i in range(devices)]

    rhos = [(None, None)]
    rho = 1.0 / SIGMA
    for _ in range(1, ITERS):
        rho_new = 1.0 / (2.0 * SIGMA - rho)
        rhos.append((rho, rho_new))
        rho = rho_new

    halo = lax.ppermute(warm_start[0], AXES, ring)
    msg, tail = pl.pallas_call(
        pack_kernel,
        out_shape=shaped(((cases, width), F32), ((rows_of(terms + 2), width), F32)),
        in_specs=[SMEM, SMEM, HBM, HBM],
        out_specs=[VMEM] * 2,
        scratch_shapes=[
            pltpu.VMEM((cases, width), F32),
            pltpu.VMEM((terms, 1, width), F32),
            pltpu.SemaphoreType.DMA((2,)),
        ],
        compiler_params=params(4),
        name="pack",
    )(active_blocks, contact_from, in_hbm(warm_start[0]), in_hbm(jnp.transpose(coarse_modes, (1, 0, 2))))
    halo_tail = lax.ppermute(tail, AXES, ring)
    high, low, own, gram_row = pl.pallas_call(
        functools.partial(first_kernel, terms),
        out_shape=shaped(
            (blocks, BF16), (blocks, BF16), ((cases, order), F32), ((1, LANES), F32)
        ),
        in_specs=[HBM, VMEM, VMEM],
        out_specs=[VMEM] * 4,
        scratch_shapes=[
            pltpu.VMEM((order, order), F32),
            pltpu.VMEM((cases, order), F32),
            pltpu.VMEM((ROWS, LANES), F32),
            pltpu.SemaphoreType.DMA((order // CHUNK,)),
        ],
        compiler_params=params(16),
        cost_estimate=pl.CostEstimate(
            flops=4 * cases * order * order, bytes_accessed=8 * order * order, transcendentals=0
        ),
        name="first",
    )(in_hbm(schur[0]), msg, tail)

    half = ((cases, width), F32)
    full = ((cases, order), F32)
    payload = ((devices, slot, LANES), F32)
    rows = ((rows_of(terms * (terms + 1) // 2), LANES), F32)
    near, far, pay_out, mult, masks, pieces = pl.pallas_call(
        functools.partial(second_kernel, terms),
        out_shape=shaped(half, half, payload, full, ((2, order), F32), ((3 * ROWS, order), BF16)),
        in_specs=[VMEM] * 9,
        out_specs=[VMEM] * 6,
        compiler_params=params(8),
        name="second",
    )(high, low, own, halo, halo_tail, msg, tail, load[0], gram_row)

    update = factor = None
    amp_scratch = [pltpu.VMEM((ROWS, LANES), F32)]
    for step in range(ITERS):
        far_in = lax.ppermute(far, AXES, far_pairs if step < ITERS - 1 else back)
        if step < ITERS - 1:
            near_in = lax.ppermute(near, AXES, near_pairs)
        gathered = lax.all_to_all(pay_out, AXES, 0, 0)
        first = step == 0
        if step < ITERS - 1:
            inputs = [gathered, near, far, near_in, far_in, mult, masks, pieces, load[0], high, low]
            outputs = [half, half, payload, full, full]
            if first:
                outputs.append(rows)
            else:
                inputs += [update, factor]
            out = pl.pallas_call(
                functools.partial(middle_kernel, terms, first, step < ITERS - 2, rhos[step]),
                out_shape=shaped(*outputs),
                in_specs=[VMEM] * len(inputs),
                out_specs=[VMEM] * len(outputs),
                scratch_shapes=amp_scratch + [pltpu.VMEM((cases, order), F32)],
                compiler_params=params(12),
            )(*inputs)
            near, far, pay_out, mult, update = out[:5]
            if first:
                factor = out[5]
        else:
            inputs = [gathered, near, far_in, mult, masks, pieces, update, factor]
            mult, residual, amplitudes = pl.pallas_call(
                functools.partial(last_kernel, terms, rhos[step]),
                out_shape=shaped(half, half, ((terms, cases), F32)),
                in_specs=[VMEM] * len(inputs),
                out_specs=[VMEM] * 3,
                scratch_shapes=amp_scratch,
                compiler_params=params(8),
                name="last",
            )(*inputs)
    return mult[None], residual[None], amplitudes.T


def solution(mesh):
    placed = (
        P(AXES, None, None),
        P(AXES, None, None),
        P(AXES, None, None),
        P(AXES, None, None),
        P(AXES),
        P(AXES),
    )
    return jax.shard_map(
        shards,
        mesh=mesh,
        in_specs=placed,
        out_specs=(P(AXES, None, None), P(AXES, None, None), P()),
        check_vma=False,
    )
```

```python
import functools
import math

import jax
import jax.numpy as jnp
from jax import lax
from jax.experimental import pallas as pl
from jax.experimental.pallas import tpu as pltpu
from jax.sharding import PartitionSpec as P

BLK = 128
ITERS = 3
LOWER = 0.1
UPPER = 8.0
THETA = (LOWER + UPPER) / 2.0
DELTA = (UPPER - LOWER) / 2.0
SIGMA = THETA / DELTA

AXES = ("group", "dev")
LANES = 128
ROWS = 8
CHUNK = 128
DEPTH = 256
WIDE = 256
LAG = 2
F32 = jnp.float32
BF16 = jnp.bfloat16
HIGHEST = lax.Precision.HIGHEST
VMEM = pl.BlockSpec(memory_space=pltpu.VMEM)
SMEM = pl.BlockSpec(memory_space=pltpu.SMEM)
HBM = pl.BlockSpec(memory_space=pltpu.HBM)


def split(x):
    high = x.astype(BF16)
    return high, (x - high.astype(F32)).astype(BF16)


def split3(x):
    high = x.astype(BF16)
    rest = x - high.astype(F32)
    middle = rest.astype(BF16)
    return high, middle, (rest - middle.astype(F32)).astype(BF16)


def dot(a, b):
    return jnp.dot(a, b, preferred_element_type=F32)


def product(x, high, low):
    cases = x.shape[0]
    x_high, x_low = split(x)
    both = dot(jnp.concatenate([x_high, x_low], axis=0), high)
    return both[:cases] + (both[cases:] + dot(x_high, low))


def block_product(both, high_ref, low_ref, start, n):
    cases, depth = both.shape[0] // 2, both.shape[1]
    at = n * (WIDE // LANES)
    high, low = (
        jnp.concatenate([ref[at + p, start : start + depth, :] for p in range(WIDE // LANES)], axis=1)
        for ref in (high_ref, low_ref)
    )
    first = dot(both, high)
    return first[:cases] + (first[cases:] + dot(both[:cases], low))


def position():
    me = lax.axis_index("group") * lax.axis_size("dev") + lax.axis_index("dev")
    return me, lax.axis_size("group") * lax.axis_size("dev")


def pack_kernel(count_ref, from_ref, warm_hbm, modes_hbm, out_ref, tail_ref, warm_ref, modes_ref, sems):
    copies = [
        pltpu.make_async_copy(source, target, sems.at[n])
        for n, (source, target) in enumerate(((warm_hbm, warm_ref), (modes_hbm, modes_ref)))
    ]
    for copy in copies:
        copy.start()
    _, width = warm_ref.shape
    terms = modes_ref.shape[0]
    spare = tail_ref.shape[0] - terms
    dofs = lax.broadcasted_iota(jnp.int32, (1, width), 1)
    alive = dofs < count_ref[0] * BLK
    live = alive.astype(F32)
    contact = (alive & (dofs >= from_ref[0])).astype(F32)
    for copy in copies:
        copy.wait()
    out_ref[...] = warm_ref[...] * live
    for c in range(terms):
        tail_ref[c : c + 1, :] = modes_ref[c] * live
    if spare > 2:
        tail_ref[terms:, :] = jnp.zeros((spare, width), F32)
    tail_ref[-2:-1, :] = live
    tail_ref[-1:, :] = contact


def first_kernel(terms, schur_ref, msg_ref, tail_ref, high_ref, low_ref, own_ref, gram_ref, raw, acc, wide, sems):
    order = schur_ref.shape[0]
    chunks = order // CHUNK
    half = chunks // 2
    sequence = list(range(half, chunks)) + list(range(half))

    def copy(c):
        rows = pl.ds(c * CHUNK, CHUNK)
        return pltpu.make_async_copy(schur_ref.at[rows, :], raw.at[rows, :], sems.at[c])

    for c in sequence:
        copy(c).start()
    modes = tail_ref[:ROWS, :]
    modes = jnp.where(lax.broadcasted_iota(jnp.int32, modes.shape, 0) < terms, modes, 0.0)
    wide[...] = jnp.zeros_like(wide)
    wide[:, :ROWS] = lax.dot_general(
        modes, modes, (((1,), (1,)), ((), ())), precision=HIGHEST, preferred_element_type=F32
    )
    row = wide[0:1, :]
    for c in range(1, terms):
        row = row + pltpu.roll(wide[c : c + 1, :], ROWS * c, 1)
    gram_ref[...] = row
    for n, c in enumerate(sequence):
        copy(c).wait()
        rows = pl.ds(c * CHUNK, CHUNK)
        high, low = split(raw[rows, :])
        for j in range(order // LANES):
            lanes = slice(j * LANES, (j + 1) * LANES)
            high_ref[j, c * CHUNK : (c + 1) * CHUNK, :] = high[:, lanes]
            low_ref[j, c * CHUNK : (c + 1) * CHUNK, :] = low[:, lanes]
        if n < half:
            part = product(msg_ref[:, n * CHUNK : (n + 1) * CHUNK], high, low)
            if n == 0:
                acc[...] = part
            else:
                acc[...] += part
    own_ref[...] = acc[...]


def finish(block, terms, even, load_ref, pieces, gram_row, near_ref, far_ref, pay_ref):
    cases, width = load_ref.shape
    count = 2 * width // WIDE
    across = (((1,), (1,)), ((), ()))
    z = []
    top = low = 0.0
    for n in range(count + LAG):
        if n < count:
            value = block(n)
            if n * WIDE >= width:
                cols = slice(n * WIDE - width, (n + 1) * WIDE - width)
                partner = z[n - count // 2]
                value = load_ref[:, cols] - value
                near_ref[:, cols] = value if even is None else jnp.where(even, value, partner)
                far_ref[:, cols] = partner if even is None else jnp.where(even, partner, value)
            z.append(value)
        if n >= LAG:
            part = pieces[:, (n - LAG) * WIDE : (n - LAG + 1) * WIDE]
            z_high, z_low = split(z[n - LAG])
            top = top + lax.dot_general(part, z_high, across, preferred_element_type=F32)
            low = low + lax.dot_general(part, z_low, across, preferred_element_type=F32)
    coef = top[:ROWS] + ((top[ROWS : 2 * ROWS] + low[:ROWS]) + (top[2 * ROWS : 3 * ROWS] + low[ROWS : 2 * ROWS]))
    per_row = LANES // cases
    used = terms // per_row
    lines = jnp.concatenate([coef[p * used : (p + 1) * used, :] for p in range(per_row)], axis=1)
    slots = pay_ref.shape[0]
    pay_ref[:, :used, :] = jnp.broadcast_to(lines[None], (slots, used, LANES))
    if gram_row is not None:
        pay_ref[:, used : used + 1, :] = jnp.broadcast_to(gram_row[None], (slots, 1, LANES))


def second_kernel(
    terms, high_ref, low_ref, own_ref, halo_ref, halo_tail_ref, msg_ref, tail_ref, load_ref, gram_ref,
    near_ref, far_ref, pay_ref, mult_ref, mask_ref, pieces_ref,
):
    me, _ = position()
    halo_tail = jnp.where(me > 0, halo_tail_ref[...], 0.0)
    left = jnp.where(halo_tail[-2:-1] > 0.0, halo_ref[...], 0.0)
    mask_ref[...] = jnp.concatenate([halo_tail[-2:], tail_ref[-2:, :]], axis=1)
    modes = jnp.concatenate([halo_tail[:ROWS], tail_ref[:ROWS, :]], axis=1)
    modes = jnp.where(lax.broadcasted_iota(jnp.int32, modes.shape, 0) < terms, modes, 0.0)
    pieces = jnp.concatenate(split3(modes), axis=0)
    pieces_ref[...] = pieces
    both = jnp.concatenate(split(left), axis=0)

    def block(n):
        return own_ref[:, n * WIDE : (n + 1) * WIDE] - block_product(both, high_ref, low_ref, 0, n)

    finish(block, terms, me % 2 == 0, load_ref, pieces, gram_ref[...], near_ref, far_ref, pay_ref)
    mult_ref[...] = jnp.concatenate([left, msg_ref[...]], axis=1)


def factor_rows(row, terms):
    def entry(c, e):
        lane = ROWS * c + e
        return jnp.broadcast_to(row[:, lane : lane + 1], (1, LANES))

    lower = {}
    inverse = []
    for j in range(terms):
        pivot = entry(j, j)
        for k in range(j):
            pivot = pivot - lower[j, k] * lower[j, k]
        root = jnp.sqrt(pivot)
        inverse.append(1.0 / root)
        for i in range(j + 1, terms):
            value = entry(i, j)
            for k in range(j):
                value = value - lower[i, k] * lower[j, k]
            lower[i, j] = value * inverse[j]
    return lower, inverse


def store_factor(lower, inverse, fac_ref):
    terms = len(inverse)
    n = 0
    for j in range(terms):
        fac_ref[n : n + 1, :] = inverse[j]
        n += 1
    for j in range(terms):
        for i in range(j + 1, terms):
            fac_ref[n : n + 1, :] = lower[i, j]
            n += 1


def load_factor(terms, fac_ref):
    inverse = [fac_ref[j : j + 1, :] for j in range(terms)]
    lower = {}
    n = terms
    for j in range(terms):
        for i in range(j + 1, terms):
            lower[i, j] = fac_ref[n : n + 1, :]
            n += 1
    return lower, inverse


def solve(total, lower, inverse, cases, amp_ref):
    terms = len(inverse)
    per_row = LANES // cases
    used = terms // per_row
    known = []
    for c in range(terms):
        row = total[c % used : c % used + 1, :]
        value = row if c < used else pltpu.roll(row, LANES - (c // used) * cases, 1)
        for k in range(c):
            value = value - lower[c, k] * known[k]
        known.append(value * inverse[c])
    for c in reversed(range(terms)):
        value = known[c]
        for k in range(c + 1, terms):
            value = value - lower[k, c] * known[k]
        known[c] = value * inverse[c]
    amp_ref[...] = jnp.zeros_like(amp_ref)
    for c in range(terms):
        amp_ref[c : c + 1, :] = known[c]
    return amp_ref[...]


def chebyshev(residual, update, rhos):
    rho, rho_new = rhos
    if rho is None:
        return residual / THETA
    return rho_new * rho * update + 2.0 * rho_new / DELTA * residual


def amplitudes_of(amp, cases):
    one, two, three = (p.astype(F32) for p in split3(amp))
    return jnp.transpose(jnp.concatenate([one, two, three, one, two, one], axis=0))[:cases].astype(BF16)


def stacked(pieces):
    m = [pieces[p * ROWS : (p + 1) * ROWS] for p in range(3)]
    return jnp.concatenate([m[0], m[0], m[0], m[1], m[1], m[2]], axis=0)


def middle_kernel(
    terms, first, pairs, rhos, sum_ref, near_ref, far_ref, near_in, far_in, mult_ref, mask_ref, pieces_ref, load_ref,
    high_ref, low_ref, *rest,
):
    if first:
        near_out, far_out, pay_ref, mult_out, upd_out, fac_out, amp_ref, coarse_ref = rest
    else:
        upd_ref, fac_ref, near_out, far_out, pay_ref, mult_out, upd_out, amp_ref, coarse_ref = rest
    cases, width = load_ref.shape
    me, devices = position()
    even = me % 2 == 0
    total = jnp.sum(sum_ref[...], axis=0)
    if first:
        used = total.shape[0] - 1
        lower, inverse = factor_rows(total[used : used + 1, :], terms)
        store_factor(lower, inverse, fac_out)
    else:
        lower, inverse = load_factor(terms, fac_ref)
    amp = amplitudes_of(solve(total, lower, inverse, cases, amp_ref), cases)
    pieces = pieces_ref[...]
    coarse_ref[...] = dot(amp, stacked(pieces))
    is_last = me == devices - 1
    y = []
    for start in range(0, 2 * width, DEPTH):
        lanes = slice(start, start + DEPTH)
        half = slice(start % width, start % width + DEPTH)
        near = near_ref[:, half] + near_in[:, half]
        far = far_ref[:, half] + jnp.where(is_last, 0.0, far_in[:, half])
        open_part = jnp.where(even, far, near) if start < width else jnp.where(even, near, far)
        open_part = jnp.where(mask_ref[0:1, lanes] > 0.0, open_part, 0.0)
        residual = open_part - coarse_ref[:, lanes]
        update = chebyshev(residual, None if first else upd_ref[:, lanes], rhos)
        mult = mult_ref[:, lanes] + update
        mult = jnp.where(mask_ref[1:2, lanes] > 0.0, jnp.maximum(mult, 0.0), mult)
        mult_out[:, lanes] = mult
        upd_out[:, lanes] = update
        both = jnp.concatenate(split(-mult if start < width else mult), axis=0)
        if start + DEPTH < 2 * width:
            parts = [block_product(both, high_ref, low_ref, start, n) for n in range(2 * width // WIDE)]
            y = [a + b for a, b in zip(y, parts)] if y else parts

    def block(n):
        return y[n] + block_product(both, high_ref, low_ref, start, n)

    finish(block, terms, even if pairs else None, load_ref, pieces, None, near_out, far_out, pay_ref)


def last_kernel(
    terms, rhos, sum_ref, own_ref, next_in, mult_ref, mask_ref, pieces_ref, upd_ref, fac_ref,
    mult_out, res_out, amp_out, amp_ref,
):
    cases, width = mult_out.shape
    me, devices = position()
    total = jnp.sum(sum_ref[...], axis=0)
    lower, inverse = load_factor(terms, fac_ref)
    amp = amplitudes_of(solve(total, lower, inverse, cases, amp_ref), cases)
    open_part = own_ref[...] + jnp.where(me == devices - 1, 0.0, next_in[...])
    live = mask_ref[0:1, width:]
    contact = mask_ref[1:2, width:] > 0.0
    open_part = jnp.where(live > 0.0, open_part, 0.0)
    residual = open_part - dot(amp, stacked(pieces_ref[:, width:]))
    res_out[...] = residual
    update = chebyshev(residual, upd_ref[:, width:], rhos)
    mult = mult_ref[:, width:] + update
    mult_out[...] = jnp.where(contact, jnp.maximum(mult, 0.0), mult)
    amp_out[...] = amp_ref[:terms, :cases]


def rows_of(count):
    return math.ceil(count / ROWS) * ROWS


def shaped(*shapes):
    return [jax.ShapeDtypeStruct(s, d) for s, d in shapes]


def in_hbm(x):
    return pltpu.with_memory_space_constraint(x, pltpu.HBM)


def params(megabytes):
    return pltpu.CompilerParams(vmem_limit_bytes=megabytes << 20)


def shards(schur, coarse_modes, load, warm_start, active_blocks, contact_from):
    _, cases, width = load.shape
    order = schur.shape[1]
    terms = coarse_modes.shape[1]
    devices = lax.axis_size("group") * lax.axis_size("dev")
    blocks = (order // LANES, order, LANES)
    slot = terms // (LANES // cases) + 1
    ring = [(i, (i + 1) % devices) for i in range(devices)]
    back = [(target, source) for source, target in ring]
    near_pairs = [(i, i ^ 1) for i in range(devices)]
    far_pairs = [(i, (i + (1 if i % 2 else devices - 1)) % devices) for i in range(devices)]

    rhos = [(None, None)]
    rho = 1.0 / SIGMA
    for _ in range(1, ITERS):
        rho_new = 1.0 / (2.0 * SIGMA - rho)
        rhos.append((rho, rho_new))
        rho = rho_new

    halo = lax.ppermute(warm_start[0], AXES, ring)
    msg, tail = pl.pallas_call(
        pack_kernel,
        out_shape=shaped(((cases, width), F32), ((rows_of(terms + 2), width), F32)),
        in_specs=[SMEM, SMEM, HBM, HBM],
        out_specs=[VMEM] * 2,
        scratch_shapes=[
            pltpu.VMEM((cases, width), F32),
            pltpu.VMEM((terms, 1, width), F32),
            pltpu.SemaphoreType.DMA((2,)),
        ],
        compiler_params=params(4),
        name="pack",
    )(active_blocks, contact_from, in_hbm(warm_start[0]), in_hbm(jnp.transpose(coarse_modes, (1, 0, 2))))
    halo_tail = lax.ppermute(tail, AXES, ring)
    high, low, own, gram_row = pl.pallas_call(
        functools.partial(first_kernel, terms),
        out_shape=shaped(
            (blocks, BF16), (blocks, BF16), ((cases, order), F32), ((1, LANES), F32)
        ),
        in_specs=[HBM, VMEM, VMEM],
        out_specs=[VMEM] * 4,
        scratch_shapes=[
            pltpu.VMEM((order, order), F32),
            pltpu.VMEM((cases, order), F32),
            pltpu.VMEM((ROWS, LANES), F32),
            pltpu.SemaphoreType.DMA((order // CHUNK,)),
        ],
        compiler_params=params(16),
        cost_estimate=pl.CostEstimate(
            flops=4 * cases * order * order, bytes_accessed=8 * order * order, transcendentals=0
        ),
        name="first",
    )(in_hbm(schur[0]), msg, tail)

    half = ((cases, width), F32)
    full = ((cases, order), F32)
    payload = ((devices, slot, LANES), F32)
    rows = ((rows_of(terms * (terms + 1) // 2), LANES), F32)
    near, far, pay_out, mult, masks, pieces = pl.pallas_call(
        functools.partial(second_kernel, terms),
        out_shape=shaped(half, half, payload, full, ((2, order), F32), ((3 * ROWS, order), BF16)),
        in_specs=[VMEM] * 9,
        out_specs=[VMEM] * 6,
        compiler_params=params(8),
        name="second",
    )(high, low, own, halo, halo_tail, msg, tail, load[0], gram_row)

    update = factor = None
    amp_scratch = [pltpu.VMEM((ROWS, LANES), F32)]
    for step in range(ITERS):
        far_in = lax.ppermute(far, AXES, far_pairs if step < ITERS - 1 else back)
        if step < ITERS - 1:
            near_in = lax.ppermute(near, AXES, near_pairs)
        gathered = lax.all_to_all(pay_out, AXES, 0, 0)
        first = step == 0
        if step < ITERS - 1:
            inputs = [gathered, near, far, near_in, far_in, mult, masks, pieces, load[0], high, low]
            outputs = [half, half, ((devices, slot - 1, LANES), F32), full, full]
            if first:
                outputs.append(rows)
            else:
                inputs += [update, factor]
            out = pl.pallas_call(
                functools.partial(middle_kernel, terms, first, step < ITERS - 2, rhos[step]),
                out_shape=shaped(*outputs),
                in_specs=[VMEM] * len(inputs),
                out_specs=[VMEM] * len(outputs),
                scratch_shapes=amp_scratch + [pltpu.VMEM((cases, order), F32)],
                compiler_params=params(12),
            )(*inputs)
            near, far, pay_out, mult, update = out[:5]
            if first:
                factor = out[5]
        else:
            inputs = [gathered, near, far_in, mult, masks, pieces, update, factor]
            mult, residual, amplitudes = pl.pallas_call(
                functools.partial(last_kernel, terms, rhos[step]),
                out_shape=shaped(half, half, ((terms, cases), F32)),
                in_specs=[VMEM] * len(inputs),
                out_specs=[VMEM] * 3,
                scratch_shapes=amp_scratch,
                compiler_params=params(8),
                name="last",
            )(*inputs)
    return mult[None], residual[None], amplitudes.T


def solution(mesh):
    placed = (
        P(AXES, None, None),
        P(AXES, None, None),
        P(AXES, None, None),
        P(AXES, None, None),
        P(AXES),
        P(AXES),
    )
    return jax.shard_map(
        shards,
        mesh=mesh,
        in_specs=placed,
        out_specs=(P(AXES, None, None), P(AXES, None, None), P()),
        check_vma=False,
    )
```

```python
import functools
import math

import jax
import jax.numpy as jnp
from jax import lax
from jax.experimental import pallas as pl
from jax.experimental.pallas import tpu as pltpu
from jax.sharding import PartitionSpec as P

BLK = 128
ITERS = 3
LOWER = 0.1
UPPER = 8.0
THETA = (LOWER + UPPER) / 2.0
DELTA = (UPPER - LOWER) / 2.0
SIGMA = THETA / DELTA

AXES = ("group", "dev")
LANES = 128
ROWS = 8
CHUNK = 128
DEPTH = 256
WIDE = 256
LAG = 2
F32 = jnp.float32
BF16 = jnp.bfloat16
HIGHEST = lax.Precision.HIGHEST
VMEM = pl.BlockSpec(memory_space=pltpu.VMEM)
SMEM = pl.BlockSpec(memory_space=pltpu.SMEM)
HBM = pl.BlockSpec(memory_space=pltpu.HBM)


def split(x):
    high = x.astype(BF16)
    return high, (x - high.astype(F32)).astype(BF16)


def split3(x):
    high = x.astype(BF16)
    rest = x - high.astype(F32)
    middle = rest.astype(BF16)
    return high, middle, (rest - middle.astype(F32)).astype(BF16)


def dot(a, b):
    return jnp.dot(a, b, preferred_element_type=F32)


def product(x, high, low):
    cases = x.shape[0]
    x_high, x_low = split(x)
    both = dot(jnp.concatenate([x_high, x_low], axis=0), high)
    return both[:cases] + (both[cases:] + dot(x_high, low))


def block_product(both, high_ref, low_ref, start, n):
    cases, depth = both.shape[0] // 2, both.shape[1]
    at = n * (WIDE // LANES)
    high, low = (
        jnp.concatenate([ref[at + p, start : start + depth, :] for p in range(WIDE // LANES)], axis=1)
        for ref in (high_ref, low_ref)
    )
    first = dot(both, high)
    return first[:cases] + (first[cases:] + dot(both[:cases], low))


def position():
    me = lax.axis_index("group") * lax.axis_size("dev") + lax.axis_index("dev")
    return me, lax.axis_size("group") * lax.axis_size("dev")


def pack_kernel(count_ref, from_ref, warm_hbm, modes_hbm, out_ref, tail_ref, warm_ref, modes_ref, sems):
    copies = [
        pltpu.make_async_copy(source, target, sems.at[n])
        for n, (source, target) in enumerate(((warm_hbm, warm_ref), (modes_hbm, modes_ref)))
    ]
    for copy in copies:
        copy.start()
    _, width = warm_ref.shape
    terms = modes_ref.shape[0]
    spare = tail_ref.shape[0] - terms
    dofs = lax.broadcasted_iota(jnp.int32, (1, width), 1)
    alive = dofs < count_ref[0] * BLK
    live = alive.astype(F32)
    contact = (alive & (dofs >= from_ref[0])).astype(F32)
    for copy in copies:
        copy.wait()
    out_ref[...] = warm_ref[...] * live
    for c in range(terms):
        tail_ref[c : c + 1, :] = modes_ref[c] * live
    if spare > 2:
        tail_ref[terms:, :] = jnp.zeros((spare, width), F32)
    tail_ref[-2:-1, :] = live
    tail_ref[-1:, :] = contact


def first_kernel(terms, schur_ref, msg_ref, tail_ref, high_ref, low_ref, own_ref, gram_ref, raw, acc, wide, sems):
    order = schur_ref.shape[0]
    chunks = order // CHUNK
    half = chunks // 2
    sequence = list(range(half, chunks)) + list(range(half))

    def copy(c):
        rows = pl.ds(c * CHUNK, CHUNK)
        return pltpu.make_async_copy(schur_ref.at[rows, :], raw.at[rows, :], sems.at[c])

    for c in sequence:
        copy(c).start()
    modes = tail_ref[:ROWS, :]
    modes = jnp.where(lax.broadcasted_iota(jnp.int32, modes.shape, 0) < terms, modes, 0.0)
    wide[...] = jnp.zeros_like(wide)
    wide[:, :ROWS] = lax.dot_general(
        modes, modes, (((1,), (1,)), ((), ())), precision=HIGHEST, preferred_element_type=F32
    )
    row = wide[0:1, :]
    for c in range(1, terms):
        row = row + pltpu.roll(wide[c : c + 1, :], ROWS * c, 1)
    gram_ref[...] = row
    for n, c in enumerate(sequence):
        copy(c).wait()
        rows = pl.ds(c * CHUNK, CHUNK)
        high, low = split(raw[rows, :])
        for j in range(order // LANES):
            lanes = slice(j * LANES, (j + 1) * LANES)
            high_ref[j, c * CHUNK : (c + 1) * CHUNK, :] = high[:, lanes]
            low_ref[j, c * CHUNK : (c + 1) * CHUNK, :] = low[:, lanes]
        if n < half:
            part = product(msg_ref[:, n * CHUNK : (n + 1) * CHUNK], high, low)
            if n == 0:
                acc[...] = part
            else:
                acc[...] += part
    own_ref[...] = acc[...]


def finish(block, terms, even, load_ref, pieces, gram_row, near_ref, far_ref, pay_ref):
    cases, width = load_ref.shape
    count = 2 * width // WIDE
    across = (((1,), (1,)), ((), ()))
    z = []
    top = low = 0.0
    for n in range(count + LAG):
        if n < count:
            value = block(n)
            if n * WIDE >= width:
                cols = slice(n * WIDE - width, (n + 1) * WIDE - width)
                partner = z[n - count // 2]
                value = load_ref[:, cols] - value
                near_ref[:, cols] = value if even is None else jnp.where(even, value, partner)
                far_ref[:, cols] = partner if even is None else jnp.where(even, partner, value)
            z.append(value)
        if n >= LAG:
            part = pieces[:, (n - LAG) * WIDE : (n - LAG + 1) * WIDE]
            z_high, z_low = split(z[n - LAG])
            top = top + lax.dot_general(part, z_high, across, preferred_element_type=F32)
            low = low + lax.dot_general(part, z_low, across, preferred_element_type=F32)
    coef = top[:ROWS] + ((top[ROWS : 2 * ROWS] + low[:ROWS]) + (top[2 * ROWS : 3 * ROWS] + low[ROWS : 2 * ROWS]))
    per_row = LANES // cases
    used = terms // per_row
    lines = jnp.concatenate([coef[p * used : (p + 1) * used, :] for p in range(per_row)], axis=1)
    slots = pay_ref.shape[0]
    pay_ref[:, :used, :] = jnp.broadcast_to(lines[None], (slots, used, LANES))
    pay_ref[:, used : used + 1, :] = jnp.broadcast_to(gram_row[None], (slots, 1, LANES))


def second_kernel(
    terms, high_ref, low_ref, own_ref, halo_ref, halo_tail_ref, msg_ref, tail_ref, load_ref, gram_ref,
    near_ref, far_ref, pay_ref, mult_ref, mask_ref, pieces_ref,
):
    me, _ = position()
    halo_tail = jnp.where(me > 0, halo_tail_ref[...], 0.0)
    left = jnp.where(halo_tail[-2:-1] > 0.0, halo_ref[...], 0.0)
    mask_ref[...] = jnp.concatenate([halo_tail[-2:], tail_ref[-2:, :]], axis=1)
    modes = jnp.concatenate([halo_tail[:ROWS], tail_ref[:ROWS, :]], axis=1)
    modes = jnp.where(lax.broadcasted_iota(jnp.int32, modes.shape, 0) < terms, modes, 0.0)
    pieces = jnp.concatenate(split3(modes), axis=0)
    pieces_ref[...] = pieces
    both = jnp.concatenate(split(left), axis=0)

    def block(n):
        return own_ref[:, n * WIDE : (n + 1) * WIDE] - block_product(both, high_ref, low_ref, 0, n)

    finish(block, terms, me % 2 == 0, load_ref, pieces, gram_ref[...], near_ref, far_ref, pay_ref)
    mult_ref[...] = jnp.concatenate([left, msg_ref[...]], axis=1)


def factor_rows(row, terms):
    def entry(c, e):
        lane = ROWS * c + e
        return jnp.broadcast_to(row[:, lane : lane + 1], (1, LANES))

    lower = {}
    inverse = []
    for j in range(terms):
        pivot = entry(j, j)
        for k in range(j):
            pivot = pivot - lower[j, k] * lower[j, k]
        root = jnp.sqrt(pivot)
        inverse.append(1.0 / root)
        for i in range(j + 1, terms):
            value = entry(i, j)
            for k in range(j):
                value = value - lower[i, k] * lower[j, k]
            lower[i, j] = value * inverse[j]
    return lower, inverse


def store_factor(lower, inverse, fac_ref):
    terms = len(inverse)
    n = 0
    for j in range(terms):
        fac_ref[n : n + 1, :] = inverse[j]
        n += 1
    for j in range(terms):
        for i in range(j + 1, terms):
            fac_ref[n : n + 1, :] = lower[i, j]
            n += 1


def load_factor(terms, fac_ref):
    inverse = [fac_ref[j : j + 1, :] for j in range(terms)]
    lower = {}
    n = terms
    for j in range(terms):
        for i in range(j + 1, terms):
            lower[i, j] = fac_ref[n : n + 1, :]
            n += 1
    return lower, inverse


def solve(total, lower, inverse, cases, amp_ref):
    terms = len(inverse)
    per_row = LANES // cases
    used = terms // per_row
    known = []
    for c in range(terms):
        row = total[c % used : c % used + 1, :]
        value = row if c < used else pltpu.roll(row, LANES - (c // used) * cases, 1)
        for k in range(c):
            value = value - lower[c, k] * known[k]
        known.append(value * inverse[c])
    for c in reversed(range(terms)):
        value = known[c]
        for k in range(c + 1, terms):
            value = value - lower[k, c] * known[k]
        known[c] = value * inverse[c]
    amp_ref[...] = jnp.zeros_like(amp_ref)
    for c in range(terms):
        amp_ref[c : c + 1, :] = known[c]
    return amp_ref[...]


def chebyshev(residual, update, rhos):
    rho, rho_new = rhos
    if rho is None:
        return residual / THETA
    return rho_new * rho * update + 2.0 * rho_new / DELTA * residual


def amplitudes_of(amp, cases):
    one, two, three = (p.astype(F32) for p in split3(amp))
    return jnp.transpose(jnp.concatenate([one, two, three, one, two, one], axis=0))[:cases].astype(BF16)


def stacked(pieces):
    m = [pieces[p * ROWS : (p + 1) * ROWS] for p in range(3)]
    return jnp.concatenate([m[0], m[0], m[0], m[1], m[1], m[2]], axis=0)


def middle_kernel(
    terms, first, pairs, rhos, sum_ref, near_ref, far_ref, near_in, far_in, mult_ref, mask_ref, pieces_ref, load_ref,
    high_ref, low_ref, *rest,
):
    if first:
        near_out, far_out, pay_ref, mult_out, upd_out, fac_out, amp_ref, coarse_ref = rest
    else:
        upd_ref, fac_ref, near_out, far_out, pay_ref, mult_out, upd_out, amp_ref, coarse_ref = rest
    cases, width = load_ref.shape
    me, devices = position()
    even = me % 2 == 0
    total = jnp.sum(sum_ref[...], axis=0)
    if first:
        used = total.shape[0] - 1
        lower, inverse = factor_rows(total[used : used + 1, :], terms)
        store_factor(lower, inverse, fac_out)
    else:
        lower, inverse = load_factor(terms, fac_ref)
    amp = amplitudes_of(solve(total, lower, inverse, cases, amp_ref), cases)
    pieces = pieces_ref[...]
    coarse_ref[...] = dot(amp, stacked(pieces))
    is_last = me == devices - 1
    y = []
    for start in range(0, 2 * width, DEPTH):
        lanes = slice(start, start + DEPTH)
        half = slice(start % width, start % width + DEPTH)
        near = near_ref[:, half] + near_in[:, half]
        far = far_ref[:, half] + jnp.where(is_last, 0.0, far_in[:, half])
        open_part = jnp.where(even, far, near) if start < width else jnp.where(even, near, far)
        open_part = jnp.where(mask_ref[0:1, lanes] > 0.0, open_part, 0.0)
        residual = open_part - coarse_ref[:, lanes]
        update = chebyshev(residual, None if first else upd_ref[:, lanes], rhos)
        mult = mult_ref[:, lanes] + update
        mult = jnp.where(mask_ref[1:2, lanes] > 0.0, jnp.maximum(mult, 0.0), mult)
        mult_out[:, lanes] = mult
        upd_out[:, lanes] = update
        y.append(jnp.concatenate(split(-mult if start < width else mult), axis=0))
    both = jnp.concatenate(y, axis=1)

    def block(n):
        return block_product(both, high_ref, low_ref, 0, n)

    no_gram = jnp.zeros((1, LANES), F32)
    finish(block, terms, even if pairs else None, load_ref, pieces, no_gram, near_out, far_out, pay_ref)


def last_kernel(
    terms, rhos, sum_ref, own_ref, next_in, mult_ref, mask_ref, pieces_ref, upd_ref, fac_ref,
    mult_out, res_out, amp_out, amp_ref,
):
    cases, width = mult_out.shape
    me, devices = position()
    total = jnp.sum(sum_ref[...], axis=0)
    lower, inverse = load_factor(terms, fac_ref)
    amp = amplitudes_of(solve(total, lower, inverse, cases, amp_ref), cases)
    open_part = own_ref[...] + jnp.where(me == devices - 1, 0.0, next_in[...])
    live = mask_ref[0:1, width:]
    contact = mask_ref[1:2, width:] > 0.0
    open_part = jnp.where(live > 0.0, open_part, 0.0)
    residual = open_part - dot(amp, stacked(pieces_ref[:, width:]))
    res_out[...] = residual
    update = chebyshev(residual, upd_ref[:, width:], rhos)
    mult = mult_ref[:, width:] + update
    mult_out[...] = jnp.where(contact, jnp.maximum(mult, 0.0), mult)
    amp_out[...] = amp_ref[:terms, :cases]


def rows_of(count):
    return math.ceil(count / ROWS) * ROWS


def shaped(*shapes):
    return [jax.ShapeDtypeStruct(s, d) for s, d in shapes]


def in_hbm(x):
    return pltpu.with_memory_space_constraint(x, pltpu.HBM)


def params(megabytes):
    return pltpu.CompilerParams(vmem_limit_bytes=megabytes << 20)


def shards(schur, coarse_modes, load, warm_start, active_blocks, contact_from):
    _, cases, width = load.shape
    order = schur.shape[1]
    terms = coarse_modes.shape[1]
    devices = lax.axis_size("group") * lax.axis_size("dev")
    blocks = (order // LANES, order, LANES)
    slot = terms // (LANES // cases) + 1
    ring = [(i, (i + 1) % devices) for i in range(devices)]
    back = [(target, source) for source, target in ring]
    near_pairs = [(i, i ^ 1) for i in range(devices)]
    far_pairs = [(i, (i + (1 if i % 2 else devices - 1)) % devices) for i in range(devices)]

    rhos = [(None, None)]
    rho = 1.0 / SIGMA
    for _ in range(1, ITERS):
        rho_new = 1.0 / (2.0 * SIGMA - rho)
        rhos.append((rho, rho_new))
        rho = rho_new

    halo = lax.ppermute(warm_start[0], AXES, ring)
    msg, tail = pl.pallas_call(
        pack_kernel,
        out_shape=shaped(((cases, width), F32), ((rows_of(terms + 2), width), F32)),
        in_specs=[SMEM, SMEM, HBM, HBM],
        out_specs=[VMEM] * 2,
        scratch_shapes=[
            pltpu.VMEM((cases, width), F32),
            pltpu.VMEM((terms, 1, width), F32),
            pltpu.SemaphoreType.DMA((2,)),
        ],
        compiler_params=params(4),
        name="pack",
    )(active_blocks, contact_from, in_hbm(warm_start[0]), in_hbm(jnp.transpose(coarse_modes, (1, 0, 2))))
    halo_tail = lax.ppermute(tail, AXES, ring)
    high, low, own, gram_row = pl.pallas_call(
        functools.partial(first_kernel, terms),
        out_shape=shaped(
            (blocks, BF16), (blocks, BF16), ((cases, order), F32), ((1, LANES), F32)
        ),
        in_specs=[HBM, VMEM, VMEM],
        out_specs=[VMEM] * 4,
        scratch_shapes=[
            pltpu.VMEM((order, order), F32),
            pltpu.VMEM((cases, order), F32),
            pltpu.VMEM((ROWS, LANES), F32),
            pltpu.SemaphoreType.DMA((order // CHUNK,)),
        ],
        compiler_params=params(16),
        cost_estimate=pl.CostEstimate(
            flops=4 * cases * order * order, bytes_accessed=8 * order * order, transcendentals=0
        ),
        name="first",
    )(in_hbm(schur[0]), msg, tail)

    half = ((cases, width), F32)
    full = ((cases, order), F32)
    payload = ((devices, slot, LANES), F32)
    rows = ((rows_of(terms * (terms + 1) // 2), LANES), F32)
    near, far, pay_out, mult, masks, pieces = pl.pallas_call(
        functools.partial(second_kernel, terms),
        out_shape=shaped(half, half, payload, full, ((2, order), F32), ((3 * ROWS, order), BF16)),
        in_specs=[VMEM] * 9,
        out_specs=[VMEM] * 6,
        compiler_params=params(8),
        name="second",
    )(high, low, own, halo, halo_tail, msg, tail, load[0], gram_row)

    update = factor = None
    amp_scratch = [pltpu.VMEM((ROWS, LANES), F32)]
    for step in range(ITERS):
        far_in = lax.ppermute(far, AXES, far_pairs if step < ITERS - 1 else back)
        if step < ITERS - 1:
            near_in = lax.ppermute(near, AXES, near_pairs)
        gathered = lax.all_to_all(pay_out, AXES, 0, 0)
        first = step == 0
        if step < ITERS - 1:
            inputs = [gathered, near, far, near_in, far_in, mult, masks, pieces, load[0], high, low]
            outputs = [half, half, payload, full, full]
            if first:
                outputs.append(rows)
            else:
                inputs += [update, factor]
            out = pl.pallas_call(
                functools.partial(middle_kernel, terms, first, step < ITERS - 2, rhos[step]),
                out_shape=shaped(*outputs),
                in_specs=[VMEM] * len(inputs),
                out_specs=[VMEM] * len(outputs),
                scratch_shapes=amp_scratch + [pltpu.VMEM((cases, order), F32)],
                compiler_params=params(12),
            )(*inputs)
            near, far, pay_out, mult, update = out[:5]
            if first:
                factor = out[5]
        else:
            inputs = [gathered, near, far_in, mult, masks, pieces, update, factor]
            mult, residual, amplitudes = pl.pallas_call(
                functools.partial(last_kernel, terms, rhos[step]),
                out_shape=shaped(half, half, ((terms, cases), F32)),
                in_specs=[VMEM] * len(inputs),
                out_specs=[VMEM] * 3,
                scratch_shapes=amp_scratch,
                compiler_params=params(8),
                name="last",
            )(*inputs)
    return mult[None], residual[None], amplitudes.T


def solution(mesh):
    placed = (
        P(AXES, None, None),
        P(AXES, None, None),
        P(AXES, None, None),
        P(AXES, None, None),
        P(AXES),
        P(AXES),
    )
    return jax.shard_map(
        shards,
        mesh=mesh,
        in_specs=placed,
        out_specs=(P(AXES, None, None), P(AXES, None, None), P()),
        check_vma=False,
    )
```
